256 devices in a mesh: expert: 32 (over z, y_lo, core), blk: 8 (over x, y_hi).
Axes of the slice: x: 4, y: 4 (y_hi: 2, y_lo: 2; y = y_hi * 2 + y_lo), z: 8, core: 2. Of those that a mesh axis runs over, the one named last changes fastest.
Arguments:
- tokens: bfloat16 [16384, 7168], P(('expert', 'blk')), may hold values from -6 to 6
- expert_ids: int32 [16384, 8], P(('expert', 'blk')), may hold values from 0 to 255, all different within a row; in each aligned block of 64 rows (0 to 63, 64 to 127, ...) at most 4 rows name the same one
- gate_weights: bfloat16 [16384, 8], P(('expert', 'blk')), may hold values from 0.099609375 to 1
- w_gate: bfloat16 [32, 7168, 2048], P('expert', None, 'blk'), may hold values from -0.0625 to 0.0625
- w_up: bfloat16 [32, 7168, 2048], P('expert', None, 'blk'), may hold values from -0.0625 to 0.0625
- w_down: bfloat16 [32, 2048, 7168], P('expert', None, 'blk'), may hold values from -0.125 to 0.125
Outputs:
- mixed_out: bfloat16 [16384, 7168], P(('expert', 'blk'))
The draws below stay inside these ranges and needn't reach their ends.
Inputs may be any that keep to these rules, and one draw needn't show every extreme that they name: `expert_ids`: each row names 8 different experts; among the 64 rows of one device no expert is named more than 4 times, a bound that some block reaches.
All inputs are finite; a program needn't handle non-finite values.
Results may differ from the reference program's by a relative error of at most 0.0057.
Values may be sent and summed in bfloat16 or wider, within the bound.
A program may use at most 64 MiB of HBM per device.

```python
import math
import jax
import jax.numpy as jnp
import numpy as np
from jax import lax

D = 7168
FF = 2048
ROUTED = 256
TOP = 8
TOK_DEV = 64
CAP = 4
EXPERTS = 32
TOKENS = 16384
N_EXPERT = 32
N_BLK = 8


def levels(key, shape, shards, smallest, largest):
    gain, own = 1.0, jax.random.fold_in(key, 6)
    for dim, shards_of in shards:
        draws = jnp.exp(jax.random.uniform(jax.random.fold_in(own, dim), (shards_of,), jnp.float32, smallest / len(shards), largest / len(shards)))
        gain = gain * jnp.repeat(draws, shape[dim] // shards_of).reshape([-1 if axis == dim else 1 for axis in range(len(shape))])
    return gain


def routed_block(rng, own, number, rows, count, top, bound, lean):
    order = jax.random.permutation(rng, count)
    packed, common = portions_of(count, rows * top, bound, lean, True), portions_of(count, rows * top, bound, lean, False)
    places = jnp.arange(count)

    def named(tallies, rotation):
        used = int((tallies > 0).sum())
        fixed = max(1, used // 4)
        shifted = fixed + (places - fixed + rotation * (used - fixed)) % max(1, count - fixed)
        return jnp.zeros((count,), jnp.int32).at[order[jnp.where(places < fixed, places, shifted)]].set(jnp.asarray(tallies, jnp.int32))

    tallies = jnp.where(number % 4 == 0, named(packed, number // 4), named(common, number - number // 4 - 1))
    mixed = jax.random.permutation(jax.random.fold_in(own, 3), count)
    source_of, receiver = mixed[0:count // 2 * 2:2], mixed[1:count // 2 * 2:2]
    room = jnp.minimum(tallies[source_of] - 1, bound - tallies[receiver]) // 2
    room = jnp.where((source_of == order[0]) | (receiver == order[0]) | (tallies[receiver] == 0), 0, jnp.maximum(room, 0))
    shifted = jax.random.randint(jax.random.fold_in(own, 4), (count // 2,), 0, 1 << 20) % (room + 1)
    tallies = tallies.at[source_of].add(-shifted).at[receiver].add(shifted)
    members = jnp.searchsorted(jnp.cumsum(tallies), jnp.arange(rows * top), side="right").astype(jnp.int32)
    table = members.reshape(top, rows).T
    table = table[jax.random.permutation(jax.random.fold_in(own, 1), rows)]
    rotation = jax.random.randint(jax.random.fold_in(own, 2), (rows, 1), 0, top)
    return jnp.take_along_axis(table, (jnp.arange(top)[None, :] + rotation) % top, axis=1)


def portions_of(count, total, bound, skew, full):
    weights = [(1 << 20) // math.isqrt(standing ** skew) + 1 for standing in range(1, count + 1)]
    largest = bound if full else min(bound, max(-(-total // count), total * weights[0] // sum(weights)))
    least = 1 if total - largest >= count - 1 else 0
    holding, rest = [largest] + [least] * (count - 1), total - largest - least * (count - 1)
    while rest > 0:
        candidates = [i for i in range(1, count) if holding[i] < largest] or [i for i in range(1, count) if holding[i] < bound]
        mass, remaining = sum([weights[i] for i in candidates]), rest
        for i in candidates:
            addition = min(bound - holding[i], max(1, remaining * weights[i] // mass), rest)
            holding[i] = holding[i] + addition
            rest = rest - addition
    return np.array(holding)


def gaussian(own_key, dims, width, most, pieces=(), kind=jnp.bfloat16):
    level = levels(own_key, dims, pieces, -0.22, 0.18) if pieces else 1.0
    drawn = jax.random.normal(own_key, dims, jnp.float32) * width * level
    return jnp.minimum(jnp.maximum(drawn, -most), most).astype(kind)


def setup_inputs(seed: int = 0) -> dict:
    keys = jax.random.split(jax.random.key(seed), 7)
    tokens = gaussian(keys[0], (TOKENS, D), 1.0, 6.0, ((0, 256),))
    expert_ids_keys = jax.random.split(jax.random.fold_in(keys[1], 1), TOKENS // TOK_DEV)
    expert_ids_turns = jax.random.permutation(jax.random.fold_in(keys[1], 3), TOKENS // TOK_DEV)
    expert_ids = jax.vmap(lambda own, number: routed_block(jax.random.fold_in(keys[1], 2), own, number, TOK_DEV, ROUTED, TOP, CAP, 2))(expert_ids_keys, expert_ids_turns).reshape((TOKENS, TOP))
    gate_weights = jnp.clip(jnp.exp(math.log(1.0) - 2.306499 * jax.random.uniform(keys[2], (TOKENS, TOP), jnp.float32) ** levels(keys[2], (TOKENS, TOP), ((0, 256),), -0.2, 0.2)), 0.099609375, 1.0).astype(jnp.bfloat16)
    w_gate = gaussian(keys[3], (EXPERTS, D, FF), D ** -0.5, 0.0625, ((0, 32), (2, 8)))
    w_up = gaussian(keys[4], (EXPERTS, D, FF), D ** -0.5, 0.0625, ((0, 32), (2, 8)))
    w_down = gaussian(keys[5], (EXPERTS, FF, D), FF ** -0.5, 0.125, ((0, 32), (2, 8)))
    return {"tokens": tokens, "expert_ids": expert_ids, "gate_weights": gate_weights, "w_gate": w_gate, "w_up": w_up, "w_down": w_down}


def reference(tokens, expert_ids, gate_weights, w_gate, w_up, w_down):
    most_rows = N_EXPERT * N_BLK * CAP
    tokens_wide = tokens.astype(jnp.float32)
    labels = jnp.arange(EXPERTS, dtype=jnp.int32)

    def one_expert(running, inputs):
        expert_label, gate_mat, up_mat, down_mat = inputs
        matches = expert_ids == expert_label
        chosen = jnp.any(matches, axis=1)
        weights = jnp.sum(jnp.where(matches, gate_weights.astype(jnp.float32), 0.0), axis=1)
        row_index = jnp.nonzero(chosen, size=most_rows, fill_value=0)[0].astype(jnp.int32)
        valid_rows = jnp.arange(most_rows) < jnp.sum(chosen.astype(jnp.int32))
        row_block = tokens_wide[row_index]
        gate_part = jnp.dot(row_block, gate_mat.astype(jnp.float32), precision=lax.Precision.HIGHEST)
        up_part = jnp.dot(row_block, up_mat.astype(jnp.float32), precision=lax.Precision.HIGHEST)
        hidden = (jax.nn.silu(gate_part) * up_part).astype(jnp.bfloat16)
        hidden = lax.optimization_barrier(hidden).astype(jnp.float32)
        outputs = jnp.dot(hidden, down_mat.astype(jnp.float32), precision=lax.Precision.HIGHEST).astype(jnp.bfloat16)
        outputs = lax.optimization_barrier(outputs).astype(jnp.float32)
        scale = jnp.where(valid_rows, weights[row_index], 0.0)
        contribution = scale[:, None] * outputs
        running = running.at[row_index].add(contribution)
        return running, None

    start = jnp.zeros(tokens.shape, jnp.float32)
    running, unused = lax.scan(one_expert, start, (labels, w_gate, w_up, w_down))
    return running.astype(jnp.bfloat16)
```

```python
import jax
import jax.numpy as jnp
from jax import lax
from jax.sharding import PartitionSpec as P

CAP = 4


def slot_tables(id_rows, gate_rows, experts, capacity):
    labels = jnp.arange(experts, dtype=jnp.int32)
    matches = id_rows[:, :, None] == labels[None, None, :]
    chosen = jnp.any(matches, axis=1)
    weights = jnp.sum(jnp.where(matches, gate_rows.astype(jnp.float32)[:, :, None], 0.0), axis=1)
    counts = chosen.astype(jnp.int32)
    before = jnp.cumsum(counts, axis=0) - counts
    places = jnp.arange(capacity, dtype=jnp.int32)
    selected = chosen[:, :, None] & (before[:, :, None] == places[None, None, :])
    selector = selected.astype(jnp.bfloat16)
    weighting = jnp.where(selected, weights[:, :, None], 0.0).astype(jnp.bfloat16)
    return (selector, weighting)


def hidden_units(row_block, gate_mat, up_mat):
    gate_part = jnp.dot(row_block, gate_mat, preferred_element_type=jnp.float32)
    up_part = jnp.dot(row_block, up_mat, preferred_element_type=jnp.float32)
    return (jax.nn.silu(gate_part) * up_part).astype(jnp.bfloat16)


def on_device(tokens, expert_ids, gate_weights, w_gate, w_up, w_down):
    gate_mat = w_gate[0]
    up_mat = w_up[0]
    down_mat = w_down[0]
    experts = lax.axis_size("expert")
    blocks = lax.axis_size("blk")
    tok_dev = tokens.shape[0]
    width = tokens.shape[1]
    selector, weighting = slot_tables(expert_ids, gate_weights, experts, CAP)
    outgoing = jnp.einsum(
        "tec,td->ecd", selector, tokens, preferred_element_type=jnp.float32
    ).astype(jnp.bfloat16)
    received = lax.all_to_all(outgoing, "expert", split_axis=0, concat_axis=0, tiled=True)
    mine = received.reshape(experts * CAP, width)
    row_block = lax.all_gather(mine, "blk", axis=0, tiled=True)
    hidden = hidden_units(row_block, gate_mat, up_mat)
    hidden_all = lax.all_gather(hidden, "blk", axis=1, tiled=True)
    slices = jnp.dot(hidden_all, down_mat, preferred_element_type=jnp.float32).astype(jnp.bfloat16)
    slices = slices.reshape(blocks, experts, CAP, -1).transpose(1, 0, 2, 3)
    slices = slices.reshape(experts, blocks * CAP, -1)
    weighting_all = lax.all_gather(
        weighting.reshape(tok_dev, experts * CAP), "blk", axis=0, tiled=True
    ).reshape(blocks, tok_dev, experts, CAP)
    returned = lax.all_to_all(slices, "expert", split_axis=0, concat_axis=0, tiled=True)
    returned = returned.reshape(experts, blocks, CAP, -1)
    partial_out = jnp.einsum(
        "btec,ebcd->btd", weighting_all, returned, preferred_element_type=jnp.float32
    ).astype(jnp.bfloat16)
    partial_out = partial_out.reshape(blocks * tok_dev, -1)
    return lax.all_to_all(partial_out, "blk", split_axis=0, concat_axis=1, tiled=True)


def solution(mesh):
    return jax.shard_map(
        on_device,
        mesh=mesh,
        in_specs=(
            P(("expert", "blk"), None),
            P(("expert", "blk"), None),
            P(("expert", "blk"), None),
            P("expert", None, "blk"),
            P("expert", None, "blk"),
            P("expert", None, "blk"),
        ),
        out_specs=P(("expert", "blk"), None),
        check_vma=False,
    )
```

```python
import functools

import jax
import jax.numpy as jnp
from jax import lax
from jax.experimental import pallas as pl
from jax.experimental.pallas import tpu as pltpu
from jax.sharding import PartitionSpec as P

CAP = 4
MESH = pl.DeviceIdType.MESH
STEPS = (0, 1, 7, 2, 6, 3, 5, 4)
NZ = 8
NG = 4
NX = 4
NB = 8
CHUNKS = 4
BF = jnp.bfloat16
F32 = jnp.float32


def slot_tables(id_rows, gate_rows, labels):
    matches = id_rows[:, :, None] == labels[None, None, :]
    chosen = jnp.any(matches, axis=1)
    weights = jnp.sum(jnp.where(matches, gate_rows.astype(F32)[:, :, None], 0.0), axis=1)
    counts = chosen.astype(jnp.int32)
    before = jnp.cumsum(counts, axis=0) - counts
    places = jnp.arange(CAP, dtype=jnp.int32)
    selected = chosen[:, :, None] & (before[:, :, None] == places[None, None, :])
    weighting = jnp.where(selected, weights[:, :, None], 0.0).astype(BF)
    return selected.astype(BF), weighting


def kernel(
    pack_ref, wt_ref, wg_ref, wu_ref, wd_ref, out_ref,
    A, B, X, H, Y, R, PB, OB, WT, WX, WGU, WD, acc, pacc,
    loc, s2s, s2r, s3s, s3r, xs, xr, hs, hr, rs, rr, ws, wr, fs, fr,
):
    e = lax.axis_index("expert")
    b = lax.axis_index("blk")
    z, g = e // NG, e % NG
    yl, co = g // 2, g % 2
    x, yh = b // 2, b % 2
    width = A.shape[-1]

    def expert_at(zz, d):
        return zz * NG + ((yl + d // 2) % 2) * 2 + (co + d % 2) % 2

    def peer(j):
        return (b + j) % NB

    barrier = pltpu.get_barrier_semaphore()
    for i in range(1, NZ * NG):
        pl.semaphore_signal(barrier, inc=1, device_id=((e + i) % (NZ * NG), b), device_id_type=MESH)
    for j in range(1, NB):
        pl.semaphore_signal(barrier, inc=1, device_id=(e, peer(j)), device_id_type=MESH)
    half_w = WGU.shape[1] // 2
    loads = [
        pltpu.make_async_copy(wg_ref, WGU.at[:, pl.ds(0, half_w)], loc.at[0]),
        pltpu.make_async_copy(wu_ref, WGU.at[:, pl.ds(half_w, half_w)], loc.at[1]),
        pltpu.make_async_copy(wd_ref, WD, loc.at[2]),
        pltpu.make_async_copy(wt_ref, WT.at[b], loc.at[3]),
        pltpu.make_async_copy(pack_ref.at[0, 0], A.at[0, 0], loc.at[4]),
        pltpu.make_async_copy(pack_ref.at[1, 0], A.at[1, 0], loc.at[5]),
    ]
    for i in (4, 5, 3, 0, 1, 2):
        loads[i].start()
    pl.semaphore_wait(barrier, NZ * NG - 1 + NB - 1)

    sent = []

    def send(src, dst, ss, rs_, ee, bb):
        copy = pltpu.make_async_remote_copy(
            src_ref=src, dst_ref=dst, send_sem=ss, recv_sem=rs_,
            device_id=(ee, bb), device_id_type=MESH,
        )
        copy.start()
        sent.append(copy)

    def arrived(dst, ss, rs_):
        pltpu.make_async_remote_copy(
            src_ref=dst, dst_ref=dst, send_sem=ss, recv_sem=rs_,
            device_id=(e, peer(1)), device_id_type=MESH,
        ).wait_recv()

    for h in range(2):
        for d in (2, 3, 1):
            send(pack_ref.at[h, d], A.at[h, d], s2s.at[h, d], s2r.at[h, d], expert_at(z, d), b)
    for j in range(1, NB):
        send(wt_ref, WT.at[b], ws.at[j], wr.at[j], e, peer(j))

    def interleave(h):
        loads[4 + h].wait()
        for d in (1, 2, 3):
            arrived(A.at[h, d], s2s.at[h, d], s2r.at[h, d])
        r = lax.broadcasted_iota(jnp.int32, (64, 64), 0)
        c = lax.broadcasted_iota(jnp.int32, (64, 64), 1)
        origin = ((r >> 2) & 3) * 16 + ((r >> 4) & 3) * 4 + (r & 3)
        perm = (c == origin).astype(F32).astype(BF)
        step = 512

        @pl.loop(0, width // step)
        def _(t):
            cols = pl.ds(pl.multiple_of(t * step, step), step)
            rows = A[h, :, :, cols].reshape(64, step)
            moved = jnp.dot(perm, rows, preferred_element_type=F32).astype(BF)
            B[pl.ds(4 * h, 4), :, cols] = moved.reshape(4, 16, step)
            if h == 0:
                X[0, b, pl.ds(0, 16), cols] = moved[:16]

        for i in range(max(1, 4 * h), 4 * h + 4):
            dst = X.at[i // 2, b, pl.ds((i % 2) * 16, 16)]
            send(B.at[i], dst, s3s.at[i], s3r.at[i], ((z + NZ - STEPS[i]) % NZ) * NG + g, b)

    right = ((x + 1) % NX) * 2
    left = ((x + NX - 1) % NX) * 2
    far = ((x + 2) % NX) * 2
    me = x * 2

    class Gather:
        def __init__(self, buf, ss, rsem):
            self.buf, self.ss, self.rs = buf, ss, rsem
            self.half = buf.shape[2] // 2

        def go(self, k, block, slot, to, part=None):
            ref = self.buf.at[k, block]
            if part is not None:
                ref = self.buf.at[k, block, pl.ds(part * self.half, self.half)]
            send(ref, ref, self.ss.at[k, slot], self.rs.at[k, slot], e, to)

        def got(self, k, block, slot, part=None):
            ref = self.buf.at[k, block]
            if part is not None:
                ref = self.buf.at[k, block, pl.ds(part * self.half, self.half)]
            arrived(ref, self.ss.at[k, slot], self.rs.at[k, slot])

        def own(self, k):
            self.go(k, b, 0, right + yh)
            self.go(k, b, 1, left + yh)
            self.go(k, b, 2, me + 1 - yh)

        def partner(self, k):
            self.got(k, me + 1 - yh, 2)
            self.go(k, me + 1 - yh, 3, right + yh)
            self.go(k, me + 1 - yh, 4, left + yh)

        def onward(self, k):
            self.got(k, left + yh, 0)
            self.go(k, left + yh, 5, right + yh, 0)
            self.got(k, right + yh, 1)
            self.go(k, right + yh, 6, left + yh, 1)
            self.got(k, left + 1 - yh, 3)
            self.go(k, left + 1 - yh, 7, right + yh, 0)
            self.got(k, right + 1 - yh, 4)
            self.go(k, right + 1 - yh, 8, left + yh, 1)

        def done(self, k):
            self.got(k, far + yh, 5, 0)
            self.got(k, far + yh, 6, 1)
            self.got(k, far + 1 - yh, 7, 0)
            self.got(k, far + 1 - yh, 8, 1)

    rows_of = Gather(X, xs, xr)
    hidden_of = Gather(H, hs, hr)

    def first(k):
        for i in (2 * k, 2 * k + 1):
            if i:
                arrived(X.at[i // 2, b, pl.ds((i % 2) * 16, 16)], s3s.at[i], s3r.at[i])
        rows_of.own(k)

    def gate_up(k):
        if k == 0:
            loads[0].wait()
            loads[1].wait()
        acc[...] = jnp.zeros_like(acc)
        step = 1024

        @pl.loop(0, width // step)
        def _(t):
            cols = pl.ds(pl.multiple_of(t * step, step), step)
            rows = X[k, :, :, cols].reshape(256, step)
            acc[...] += jnp.dot(rows, WGU[cols, :], preferred_element_type=F32)

        gate, up = acc[:, :half_w], acc[:, half_w:]
        H[k, b] = (gate / (1.0 + jnp.exp(-gate)) * up).astype(BF)

    def down(k):
        if k == 0:
            loads[2].wait()
        n = WD.shape[1]
        r = lax.broadcasted_iota(jnp.int32, (256, 256), 0)
        c = lax.broadcasted_iota(jnp.int32, (256, 256), 1)
        origin = ((r >> 2) & 7) * 32 + ((r >> 7) & 1) * 16 + ((r >> 5) & 3) * 4 + (r & 3)
        perm = (c == origin).astype(F32).astype(BF)
        pacc[pl.ds(0, 256), :] = jnp.zeros((256, n), F32)

        @pl.loop(0, NB)
        def _(q):
            part = WD[pl.ds(pl.multiple_of(q * 256, 256), 256), :]
            pacc[pl.ds(0, 256), :] += jnp.dot(H[k, q], part, preferred_element_type=F32)

        rows = pacc[pl.ds(0, 256), :].astype(BF)
        moved = jnp.dot(perm, rows, preferred_element_type=F32).astype(BF)
        Y[k] = moved.reshape(8, 32, n)
        if k == 0:
            R[0, 0] = moved[:32]
        for q in range(8):
            i, d = 2 * k + q // 4, q % 4
            if i or d:
                send(Y.at[k, q], R.at[k, q], rs.at[k, q], rr.at[k, q], expert_at((z + STEPS[i]) % NZ, d), b)

    def weights():
        loads[3].wait()
        for j in range(1, NB):
            arrived(WT.at[peer(j)], ws.at[j], wr.at[NB - j])
        r = lax.broadcasted_iota(jnp.int32, (128, 1024), 0)
        c = lax.broadcasted_iota(jnp.int32, (128, 1024), 1)
        same = r == ((c >> 5) * 4 + (c & 3))

        @pl.loop(0, NB)
        def _(q):
            spread = jnp.where(same & (((c >> 2) & 7) == q), 1.0, 0.0).astype(BF)
            wide = jnp.dot(WT[q], spread, preferred_element_type=F32).astype(BF)
            WX[pl.ds(pl.multiple_of(q * 64, 64), 64), :] = wide

    def combine(k):
        for q in range(8):
            if k or q:
                arrived(R.at[k, q], rs.at[k, q], rr.at[k, q])
        n = WD.shape[1]
        part = WX[:, k * 256 : (k + 1) * 256]
        term = jnp.dot(part, R[k].reshape(256, n), preferred_element_type=F32)
        if k == 0:
            pacc[...] = term
        else:
            pacc[...] += term

    interleave(0)
    first(0)
    interleave(1)
    first(1)
    rows_of.partner(0)
    rows_of.onward(0)
    rows_of.partner(1)
    first(2)
    weights()
    for k in range(CHUNKS):
        rows_of.done(k)
        gate_up(k)
        hidden_of.own(k)
        if k + 1 < CHUNKS:
            rows_of.onward(k + 1)
        if k + 2 < CHUNKS:
            rows_of.partner(k + 2)
        if k + 3 < CHUNKS:
            first(k + 3)
        hidden_of.partner(k)
        hidden_of.onward(k)
        if k:
            hidden_of.done(k - 1)
            down(k - 1)
    hidden_of.done(CHUNKS - 1)
    down(CHUNKS - 1)
    for k in range(CHUNKS):
        combine(k)
    for q in range(NB):
        PB[q] = pacc[q * 64 : (q + 1) * 64, :].astype(BF)
    for j in range(1, NB):
        send(PB.at[peer(j)], OB.at[b], fs.at[j], fr.at[j], e, peer(j))
    OB[b] = PB[b]
    for j in range(1, NB):
        arrived(OB.at[peer(j)], fs.at[j], fr.at[NB - j])
    n = WD.shape[1]
    for q in range(NB):
        out_ref[:, q * n : (q + 1) * n] = OB[q]
    for copy in sent:
        copy.wait_send()


def on_device(tokens, expert_ids, gate_weights, w_gate, w_up, w_down):
    tok, width = tokens.shape
    half_w = w_gate.shape[2]
    full_w, n = w_down.shape[1:]
    e = lax.axis_index("expert")
    z, g = e // NG, e % NG
    steps = jnp.array(STEPS, jnp.int32)
    d = jnp.arange(NG, dtype=jnp.int32)
    quad = ((g // 2 + d // 2) % 2) * 2 + (g % 2 + d % 2) % 2
    labels = (((z + NZ - steps) % NZ)[:, None] * NG + quad[None, :]).reshape(-1)
    selector, weighting = slot_tables(expert_ids, gate_weights, labels)
    selector = selector.reshape(tok, 2, 4, NG, CAP).transpose(1, 3, 2, 4, 0).reshape(128, tok)
    packed = jnp.dot(selector, tokens, preferred_element_type=F32).astype(BF)
    packed = packed.reshape(2, NG, 16, width)
    weighting = weighting.reshape(tok, 128)
    dma = pltpu.SemaphoreType.DMA
    any_ = pl.BlockSpec(memory_space=pl.ANY)
    return pl.pallas_call(
        kernel,
        out_shape=jax.ShapeDtypeStruct((tok, width), BF),
        in_specs=[any_] * 5,
        out_specs=pl.BlockSpec(memory_space=pltpu.VMEM),
        scratch_shapes=[
            pltpu.VMEM((2, NG, 16, width), BF),
            pltpu.VMEM((NZ, 16, width), BF),
            pltpu.VMEM((CHUNKS, NB, 32, width), BF),
            pltpu.VMEM((CHUNKS, NB, 256, half_w), BF),
            pltpu.VMEM((CHUNKS, 8, 32, n), BF),
            pltpu.VMEM((CHUNKS, 8, 32, n), BF),
            pltpu.VMEM((NB, tok, n), BF),
            pltpu.VMEM((NB, tok, n), BF),
            pltpu.VMEM((NB, tok, 128), BF),
            pltpu.VMEM((NB * tok, 1024), BF),
            pltpu.VMEM((width, 2 * half_w), BF),
            pltpu.VMEM((full_w, n), BF),
            pltpu.VMEM((256, 2 * half_w), F32),
            pltpu.VMEM((NB * tok, n), F32),
            dma((6,)),
            dma((2, NG)), dma((2, NG)),
            dma((NZ,)), dma((NZ,)),
            dma((CHUNKS, 9)), dma((CHUNKS, 9)),
            dma((CHUNKS, 9)), dma((CHUNKS, 9)),
            dma((CHUNKS, 8)), dma((CHUNKS, 8)),
            dma((NB,)), dma((NB,)),
            dma((NB,)), dma((NB,)),
        ],
        compiler_params=pltpu.CompilerParams(
            collective_id=0, has_side_effects=True, vmem_limit_bytes=60 * 1024 * 1024
        ),
    )(packed, weighting, w_gate[0], w_up[0], w_down[0])


def solution(mesh):
    return jax.shard_map(
        on_device,
        mesh=mesh,
        in_specs=(
            P(("expert", "blk"), None),
            P(("expert", "blk"), None),
            P(("expert", "blk"), None),
            P("expert", None, "blk"),
            P("expert", None, "blk"),
            P("expert", None, "blk"),
        ),
        out_specs=P(("expert", "blk"), None),
        check_vma=False,
    )
```

```python
import functools

import jax
import jax.numpy as jnp
from jax import lax
from jax.experimental import pallas as pl
from jax.experimental.pallas import tpu as pltpu
from jax.sharding import PartitionSpec as P

CAP = 4
MESH = pl.DeviceIdType.MESH
STEPS = (0, 2, 4, 5, 3, 6, 1, 7)
XFIRST = (2, 4)
CHUNKS = ((0, 2), (2, 2), (4, 2), (6, 1), (7, 1))
DIRECT = (3, 4)
NZ = 8
NG = 4
NX = 4
NB = 8
BF = jnp.bfloat16
F32 = jnp.float32


def kernel(
    tok_ref, ids_ref, gw_ref, wg_ref, wu_ref, wd_ref, out_ref,
    TK, IDS, GW, O, A, B, X, H, Y, R, PB, OB, WO, WT, WX, WGU, WD, acc, pacc,
    loc, s2s, s2r, s3s, s3r, xs, xr, hs, hr, rs, rr, ws, wr, fs, fr,
):
    e = lax.axis_index("expert")
    b = lax.axis_index("blk")
    z, g = e // NG, e % NG
    yl, co = g // 2, g % 2
    x, yh = b // 2, b % 2
    width = A.shape[-1]
    half_c = width // 2
    half_w = WGU.shape[1] // 2
    n = WD.shape[1]

    def expert_at(zz, d):
        return zz * NG + ((yl + d // 2) % 2) * 2 + (co + d % 2) % 2

    def peer(j):
        return (b + j) % NB

    barrier = pltpu.get_barrier_semaphore()
    loads = [
        pltpu.make_async_copy(ids_ref, IDS, loc.at[0]),
        pltpu.make_async_copy(gw_ref, GW, loc.at[1]),
        pltpu.make_async_copy(tok_ref, TK, loc.at[2]),
        pltpu.make_async_copy(wg_ref, WGU.at[:, pl.ds(0, half_w)], loc.at[3]),
        pltpu.make_async_copy(wu_ref, WGU.at[:, pl.ds(half_w, half_w)], loc.at[4]),
        pltpu.make_async_copy(wd_ref, WD, loc.at[5]),
    ]
    for copy in loads:
        copy.start()
    for i in range(1, NZ * NG):
        pl.semaphore_signal(barrier, inc=1, device_id=((e + i) % (NZ * NG), b), device_id_type=MESH)
    for j in range(1, NB):
        pl.semaphore_signal(barrier, inc=1, device_id=(e, peer(j)), device_id_type=MESH)

    def label_of(unit, d):
        step = sum(jnp.where(unit == i, s, 0) for i, s in enumerate(STEPS))
        return ((z + NZ - step) & 7) * NG + ((yl + (d >> 1)) & 1) * 2 + ((co + d) & 1)

    def chosen_of(labels, place):
        ids = IDS[...]
        gate = GW[...].astype(F32)
        hit = jnp.zeros((ids.shape[0], 128), F32)
        weight = jnp.zeros((ids.shape[0], 128), F32)
        for j in range(ids.shape[1]):
            match = ids[:, j : j + 1] == labels
            hit = jnp.where(match, 1.0, hit)
            weight = jnp.where(match, gate[:, j : j + 1], weight)
        r = lax.broadcasted_iota(jnp.int32, (ids.shape[0], ids.shape[0]), 0)
        c = lax.broadcasted_iota(jnp.int32, (ids.shape[0], ids.shape[0]), 1)
        earlier = jnp.where(c < r, 1.0, 0.0).astype(BF)
        before = jnp.dot(earlier, hit.astype(BF), preferred_element_type=F32)
        used = (hit > 0.5) & (before == place.astype(F32))
        return jnp.where(used, 1.0, 0.0), jnp.where(used, weight, 0.0)

    loads[0].wait()
    loads[1].wait()
    col = lax.broadcasted_iota(jnp.int32, (1, 128), 1)
    selector, _ = chosen_of(label_of((col >> 6) * 4 + ((col >> 2) & 3), (col >> 4) & 3), col & 3)
    selector = selector.T.astype(BF)
    _, weighting = chosen_of(label_of(col >> 4, (col >> 2) & 3), col & 3)
    WO[...] = weighting.astype(BF)
    WT[b] = weighting.astype(BF)
    loads[2].wait()

    def pack(h, c):
        step = 512

        @pl.loop(0, half_c // step)
        def _(t):
            cols = pl.ds(pl.multiple_of(c * half_c + t * step, step), step)
            rows = jnp.dot(selector[h * 64 : h * 64 + 64], TK[:, cols], preferred_element_type=F32)
            rows = rows.astype(BF).reshape(NG, 16, step)
            O[h, :, :, cols] = rows
            A[h, 0, :, cols] = rows[0]

    for h in range(2):
        for c in range(2):
            pack(h, c)
    pl.semaphore_wait(barrier, NZ * NG - 1 + NB - 1)

    sent = []

    def send(src, dst, ss, rs_, ee, bb):
        copy = pltpu.make_async_remote_copy(
            src_ref=src, dst_ref=dst, send_sem=ss, recv_sem=rs_,
            device_id=(ee, bb), device_id_type=MESH,
        )
        copy.start()
        sent.append(copy)

    def arrived(dst, ss, rs_):
        pltpu.make_async_remote_copy(
            src_ref=dst, dst_ref=dst, send_sem=ss, recv_sem=rs_,
            device_id=(e, peer(1)), device_id_type=MESH,
        ).wait_recv()

    def side(c):
        return pl.ds(c * half_c, half_c)

    for h in range(2):
        for c in range(2):
            for d in (2, 3, 1):
                send(
                    O.at[h, d, :, side(c)], A.at[h, d, :, side(c)],
                    s2s.at[h, c, d], s2r.at[h, c, d], expert_at(z, d), b,
                )

    def interleave(h, c):
        for d in (1, 2, 3):
            arrived(A.at[h, d, :, side(c)], s2s.at[h, c, d], s2r.at[h, c, d])
        r = lax.broadcasted_iota(jnp.int32, (64, 64), 0)
        q = lax.broadcasted_iota(jnp.int32, (64, 64), 1)
        origin = ((r >> 2) & 3) * 16 + ((r >> 4) & 3) * 4 + (r & 3)
        perm = (q == origin).astype(F32).astype(BF)
        step = 512

        @pl.loop(0, half_c // step)
        def _(t):
            cols = pl.ds(pl.multiple_of(c * half_c + t * step, step), step)
            rows = A[h, :, :, cols].reshape(64, step)
            moved = jnp.dot(perm, rows, preferred_element_type=F32).astype(BF)
            B[pl.ds(4 * h, 4), :, cols] = moved.reshape(4, 16, step)
            if h == 0:
                X[0, b, :, cols] = moved[:16]

    def along_z(h):
        for i in range(max(1, 4 * h), 4 * h + 4):
            send(
                B.at[i], X.at[i, b], s3s.at[i], s3r.at[i],
                ((z + NZ - STEPS[i]) % NZ) * NG + g, b,
            )

    right = ((x + 1) % NX) * 2
    left = ((x + NX - 1) % NX) * 2
    far = ((x + 2) % NX) * 2
    me = x * 2
    other = 1 - yh

    def go(i, block, slot, to, c=None):
        ref = X.at[i, block] if c is None else X.at[i, block, :, side(c)]
        send(ref, ref, xs.at[i, slot], xr.at[i, slot], e, to)

    def got(i, block, slot, c=None):
        ref = X.at[i, block] if c is None else X.at[i, block, :, side(c)]
        arrived(ref, xs.at[i, slot], xr.at[i, slot])

    def own_side(i, c):
        go(i, b, 0 + c, right + yh, c)
        go(i, b, 2 + c, left + yh, c)
        if i not in XFIRST:
            go(i, b, 4 + c, me + other, c)

    def own(i):
        arrived(X.at[i, b], s3s.at[i], s3r.at[i])
        if i in XFIRST:
            go(i, b, 4, me + other)
        go(i, b, 0, right + yh, 0)
        go(i, b, 3, left + yh, 1)
        if i not in XFIRST:
            go(i, b, 4, me + other, 0)
            go(i, b, 5, me + other, 1)
        go(i, b, 1, right + yh, 1)
        go(i, b, 2, left + yh, 0)

    def part(i):
        if i in XFIRST:
            return
        got(i, me + other, 4, 0)
        go(i, me + other, 6, right + other_row, 0)
        got(i, me + other, 5, 1)
        go(i, me + other, 9, left + other_row, 1)
        go(i, me + other, 7, right + other_row, 1)
        go(i, me + other, 8, left + other_row, 0)

    other_row = yh

    def onward(i):
        got(i, left + yh, 0, 0)
        go(i, left + yh, 10, right + yh, 0)
        got(i, right + yh, 3, 1)
        go(i, right + yh, 11, left + yh, 1)
        if i in XFIRST:
            got(i, left + yh, 1, 1)
            go(i, left + yh, 5, me + other)
            got(i, right + yh, 2, 0)
            go(i, right + yh, 6, me + other)
        else:
            got(i, left + other, 6, 0)
            go(i, left + other, 12, right + yh, 0)
            got(i, right + other, 9, 1)
            go(i, right + other, 13, left + yh, 1)

    def done(i):
        got(i, far + yh, 10, 0)
        got(i, far + yh, 11, 1)
        if i in XFIRST:
            go(i, far + yh, 7, me + other)
            got(i, me + other, 4)
            got(i, left + other, 5)
            got(i, right + other, 6)
            got(i, far + other, 7)
        else:
            got(i, left + yh, 1, 1)
            got(i, right + yh, 2, 0)
            got(i, left + other, 7, 1)
            got(i, right + other, 8, 0)
            got(i, far + other, 12, 0)
            got(i, far + other, 13, 1)

    def h_ref(k, block, part_=None):
        i0, m = CHUNKS[k]
        if part_ is None:
            return H.at[pl.ds(i0, m), block]
        return H.at[pl.ds(i0, m), block, pl.ds(part_ * 64, 64)]

    def h_go(k, block, slot, to, part_=None):
        ref = h_ref(k, block, part_)
        send(ref, ref, hs.at[k, slot], hr.at[k, slot], e, to)

    def h_got(k, block, slot, part_=None):
        arrived(h_ref(k, block, part_), hs.at[k, slot], hr.at[k, slot])

    def h_own(k):
        if k in DIRECT:
            for j in (4, 3, 5, 2, 6, 1, 7):
                h_go(k, b, j, peer(j))
            return
        h_go(k, b, 2, me + other)
        h_go(k, b, 0, right + yh)
        h_go(k, b, 1, left + yh)

    def h_part(k):
        if k in DIRECT:
            return
        h_got(k, me + other, 2)
        h_go(k, me + other, 3, right + yh)
        h_go(k, me + other, 4, left + yh)

    def h_onward(k):
        if k in DIRECT:
            return
        h_got(k, left + yh, 0)
        h_go(k, left + yh, 5, right + yh, 0)
        h_got(k, right + yh, 1)
        h_go(k, right + yh, 6, left + yh, 1)
        h_got(k, left + other, 3)
        h_go(k, left + other, 7, right + yh, 0)
        h_got(k, right + other, 4)
        h_go(k, right + other, 8, left + yh, 1)

    def h_done(k):
        if k in DIRECT:
            for j in range(1, NB):
                h_got(k, peer(j), NB - j)
            return
        h_got(k, far + yh, 5, 0)
        h_got(k, far + yh, 6, 1)
        h_got(k, far + other, 7, 0)
        h_got(k, far + other, 8, 1)

    def gate_up(k):
        if k == 0:
            loads[3].wait()
            loads[4].wait()
        i0, m = CHUNKS[k]
        size = m * 128
        step = 1792

        @pl.loop(0, width // step)
        def _(t):
            cols = pl.ds(pl.multiple_of(t * step, step), step)
            rows = X[i0 : i0 + m, :, :, cols].reshape(size, step)
            term = jnp.dot(rows, WGU[cols, :], preferred_element_type=F32)

            @pl.when(t == 0)
            def _():
                acc[:size] = term

            @pl.when(t > 0)
            def _():
                acc[:size] += term

        gate, up = acc[:size, :half_w], acc[:size, half_w:]
        hidden = (gate / (1.0 + jnp.exp(-gate)) * up).astype(BF)
        H[i0 : i0 + m, b] = hidden.reshape(m, 128, half_w)

    def down(k):
        if k == 0:
            loads[5].wait()
        i0, m = CHUNKS[k]
        size = m * 128
        r = lax.broadcasted_iota(jnp.int32, (128, 128), 0)
        c = lax.broadcasted_iota(jnp.int32, (128, 128), 1)
        origin = ((r >> 2) & 7) * 16 + ((r >> 5) & 3) * 4 + (r & 3)
        perm = (c == origin).astype(F32).astype(BF)
        total = None
        for q in range(NB):
            term = jnp.dot(
                H[i0 : i0 + m, q].reshape(size, half_w),
                WD[q * half_w : (q + 1) * half_w, :],
                preferred_element_type=F32,
            )
            total = term if total is None else total + term
        rows = total.astype(BF)
        for u in range(m):
            i = i0 + u
            moved = jnp.dot(perm, rows[u * 128 : (u + 1) * 128], preferred_element_type=F32).astype(BF)
            Y[i] = moved.reshape(NG, 32, n)
            if i == 0:
                R[0, 0] = moved[:32]
            for d in (3, 2, 1, 0):
                if i or d:
                    send(
                        Y.at[i, d], R.at[i, d], rs.at[i, d], rr.at[i, d],
                        expert_at((z + STEPS[i]) % NZ, d), b,
                    )

    def weights():
        for j in range(1, NB):
            arrived(WT.at[peer(j)], ws.at[j], wr.at[NB - j])
        r = lax.broadcasted_iota(jnp.int32, (128, 1024), 0)
        c = lax.broadcasted_iota(jnp.int32, (128, 1024), 1)
        same = r == ((c >> 5) * 4 + (c & 3))

        @pl.loop(0, NB)
        def _(q):
            spread = jnp.where(same & (((c >> 2) & 7) == q), 1.0, 0.0).astype(BF)
            wide = jnp.dot(WT[q], spread, preferred_element_type=F32).astype(BF)
            WX[pl.ds(pl.multiple_of(q * 64, 64), 64), :] = wide

    def combine(k):
        i0, m = CHUNKS[k]
        for i in range(i0, i0 + m):
            for d in range(NG):
                if i or d:
                    arrived(R.at[i, d], rs.at[i, d], rr.at[i, d])
        part_ = WX[:, i0 * 128 : (i0 + m) * 128]
        term = jnp.dot(part_, R[i0 : i0 + m].reshape(m * 128, n), preferred_element_type=F32)
        if k == 0:
            pacc[...] = term
        elif k + 1 < len(CHUNKS):
            pacc[...] += term
        else:
            PB[...] = (pacc[...] + term).astype(BF).reshape(NB, 64, n)

    interleave(0, 0)
    own_side(0, 0)
    interleave(0, 1)
    own_side(0, 1)
    along_z(0)
    for j in range(1, NB):
        send(WO, WT.at[b], ws.at[j], wr.at[j], e, peer(j))
    part(0)
    interleave(1, 0)
    interleave(1, 1)
    along_z(1)
    own(1)
    onward(0)
    part(1)
    own(2)
    weights()
    for t in range(1, 9):
        if t + 2 < 8:
            own(t + 2)
        if t + 1 < 8:
            part(t + 1)
        if t < 8:
            onward(t)
        if t == 3:
            h_part(0)
        if t == 5:
            h_part(1)
        if t == 7:
            h_part(2)
        done(t - 1)
        if t == 2:
            gate_up(0)
            h_own(0)
        if t == 3:
            h_onward(0)
        if t == 4:
            gate_up(1)
            h_own(1)
            h_done(0)
            down(0)
        if t == 5:
            h_onward(1)
        if t == 6:
            gate_up(2)
            h_own(2)
            h_done(1)
            down(1)
            combine(0)
        if t == 7:
            h_onward(2)
            gate_up(3)
            h_own(3)
        if t == 8:
            gate_up(4)
            h_own(4)
            h_done(2)
            down(2)
            h_done(3)
            down(3)
            h_done(4)
            down(4)
    for k in range(1, 5):
        combine(k)
    for j in (4, 3, 5, 2, 6, 1, 7):
        send(PB.at[peer(j)], OB.at[b], fs.at[j], fr.at[j], e, peer(j))
    OB[b] = PB[b]
    for j in range(1, NB):
        arrived(OB.at[peer(j)], fs.at[j], fr.at[NB - j])
    for q in range(NB):
        out_ref[:, q * n : (q + 1) * n] = OB[q]
    for copy in sent:
        copy.wait_send()


def on_device(tokens, expert_ids, gate_weights, w_gate, w_up, w_down):
    tok, width = tokens.shape
    half_w = w_gate.shape[2]
    full_w, n = w_down.shape[1:]
    dma = pltpu.SemaphoreType.DMA
    any_ = pl.BlockSpec(memory_space=pl.ANY)
    units = NZ
    return pl.pallas_call(
        kernel,
        out_shape=jax.ShapeDtypeStruct((tok, width), BF),
        in_specs=[any_] * 6,
        out_specs=pl.BlockSpec(memory_space=pltpu.VMEM),
        scratch_shapes=[
            pltpu.VMEM((tok, width), BF),
            pltpu.VMEM(expert_ids.shape, jnp.int32),
            pltpu.VMEM(gate_weights.shape, BF),
            pltpu.VMEM((2, NG, 16, width), BF),
            pltpu.VMEM((2, NG, 16, width), BF),
            pltpu.VMEM((units, 16, width), BF),
            pltpu.VMEM((units, NB, 16, width), BF),
            pltpu.VMEM((units, NB, 128, half_w), BF),
            pltpu.VMEM((units, NG, 32, n), BF),
            pltpu.VMEM((units, NG, 32, n), BF),
            pltpu.VMEM((NB, tok, n), BF),
            pltpu.VMEM((NB, tok, n), BF),
            pltpu.VMEM((tok, 128), BF),
            pltpu.VMEM((NB, tok, 128), BF),
            pltpu.VMEM((NB * tok, 1024), BF),
            pltpu.VMEM((width, 2 * half_w), BF),
            pltpu.VMEM((full_w, n), BF),
            pltpu.VMEM((256, 2 * half_w), F32),
            pltpu.VMEM((NB * tok, n), F32),
            dma((6,)),
            dma((2, 2, NG)), dma((2, 2, NG)),
            dma((units,)), dma((units,)),
            dma((units, 14)), dma((units, 14)),
            dma((len(CHUNKS), 9)), dma((len(CHUNKS), 9)),
            dma((units, NG)), dma((units, NG)),
            dma((NB,)), dma((NB,)),
            dma((NB,)), dma((NB,)),
        ],
        compiler_params=pltpu.CompilerParams(
            collective_id=0, has_side_effects=True, vmem_limit_bytes=63 * 1024 * 1024
        ),
    )(tokens, expert_ids, gate_weights, w_gate[0], w_up[0], w_down[0])


def solution(mesh):
    return jax.shard_map(
        on_device,
        mesh=mesh,
        in_specs=(
            P(("expert", "blk"), None),
            P(("expert", "blk"), None),
            P(("expert", "blk"), None),
            P("expert", None, "blk"),
            P("expert", None, "blk"),
            P("expert", None, "blk"),
        ),
        out_specs=P(("expert", "blk"), None),
        check_vma=False,
    )
```

```python
import functools

import jax
import jax.numpy as jnp
from jax import lax
from jax.experimental import pallas as pl
from jax.experimental.pallas import tpu as pltpu
from jax.sharding import PartitionSpec as P

CAP = 4
MESH = pl.DeviceIdType.MESH
STEPS = (0, 1, 4, 5, 3, 6, 2, 7)
XFIRST = (2, 4)
CHUNKS = ((0, 2), (2, 2), (4, 2), (6, 1), (7, 1))
DIRECT = (3, 4)
NZ = 8
NG = 4
NX = 4
NB = 8
BF = jnp.bfloat16
F32 = jnp.float32


def kernel(
    tok_ref, ids_ref, gw_ref, wg_ref, wu_ref, wd_ref, out_ref,
    TK, IDS, GW, O, A, B, X, H, Y, R, PB, OB, WO, WT, WX, WGU, WD, acc, pacc,
    loc, s2s, s2r, s3s, s3r, xs, xr, hs, hr, rs, rr, ws, wr, fs, fr,
):
    e = lax.axis_index("expert")
    b = lax.axis_index("blk")
    z, g = e // NG, e % NG
    yl, co = g // 2, g % 2
    x, yh = b // 2, b % 2
    width = A.shape[-1]
    half_c = width // 2
    half_w = WGU.shape[1] // 2
    n = WD.shape[1]

    def expert_at(zz, d):
        return zz * NG + ((yl + d // 2) % 2) * 2 + (co + d % 2) % 2

    def peer(j):
        return (b + j) % NB

    barrier = pltpu.get_barrier_semaphore()
    loads = [
        pltpu.make_async_copy(ids_ref, IDS, loc.at[0]),
        pltpu.make_async_copy(gw_ref, GW, loc.at[1]),
        pltpu.make_async_copy(tok_ref, TK, loc.at[2]),
        pltpu.make_async_copy(wg_ref, WGU.at[:, pl.ds(0, half_w)], loc.at[3]),
        pltpu.make_async_copy(wu_ref, WGU.at[:, pl.ds(half_w, half_w)], loc.at[4]),
        pltpu.make_async_copy(wd_ref, WD, loc.at[5]),
    ]
    for copy in loads[:3]:
        copy.start()
    for d in range(1, NG):
        pl.semaphore_signal(barrier, inc=1, device_id=(expert_at(z, d), b), device_id_type=MESH)
    for i in range(1, NZ):
        pl.semaphore_signal(barrier, inc=1, device_id=((z + i) % NZ * NG + g, b), device_id_type=MESH)
    near = (((x + 1) % NX) * 2 + yh, ((x + NX - 1) % NX) * 2 + yh, x * 2 + 1 - yh)
    for block in near:
        pl.semaphore_signal(barrier, inc=1, device_id=(e, block), device_id_type=MESH)

    def label_of(unit, d):
        step = sum(jnp.where(unit == i, s, 0) for i, s in enumerate(STEPS))
        return ((z + NZ - step) & 7) * NG + ((yl + (d >> 1)) & 1) * 2 + ((co + d) & 1)

    def chosen_of(labels, place):
        ids = IDS[...]
        gate = GW[...].astype(F32)
        tok = ids.shape[1]
        hit = jnp.zeros((128, tok), F32)
        weight = jnp.zeros((128, tok), F32)
        for j in range(ids.shape[0]):
            match = ids[j : j + 1] == labels
            hit = jnp.where(match, 1.0, hit)
            weight = jnp.where(match, gate[j : j + 1], weight)
        r = lax.broadcasted_iota(jnp.int32, (tok, tok), 0)
        c = lax.broadcasted_iota(jnp.int32, (tok, tok), 1)
        earlier = jnp.where(r < c, 1.0, 0.0).astype(BF)
        before = jnp.dot(hit.astype(BF), earlier, preferred_element_type=F32)
        used = (hit > 0.5) & (before == place.astype(F32))
        return jnp.where(used, 1.0, 0.0), jnp.where(used, weight, 0.0)

    loads[0].wait()
    loads[1].wait()
    row = lax.broadcasted_iota(jnp.int32, (128, 1), 0)
    selector, _ = chosen_of(label_of((row >> 6) * 4 + ((row >> 2) & 3), (row >> 4) & 3), row & 3)
    selector = selector.astype(BF)
    loads[2].wait()

    def pack(h, c):
        step = 512

        @pl.loop(0, half_c // step)
        def _(t):
            cols = pl.ds(pl.multiple_of(c * half_c + t * step, step), step)
            rows = jnp.dot(selector[h * 64 : h * 64 + 64], TK[:, cols], preferred_element_type=F32)
            rows = rows.astype(BF).reshape(NG, 16, step)
            O[h, :, :, cols] = rows
            A[h, 0, :, cols] = rows[0]

    sent = []

    def send(src, dst, ss, rs_, ee, bb):
        copy = pltpu.make_async_remote_copy(
            src_ref=src, dst_ref=dst, send_sem=ss, recv_sem=rs_,
            device_id=(ee, bb), device_id_type=MESH,
        )
        copy.start()
        sent.append(copy)

    def arrived(dst, ss, rs_):
        pltpu.make_async_remote_copy(
            src_ref=dst, dst_ref=dst, send_sem=ss, recv_sem=rs_,
            device_id=(e, peer(1)), device_id_type=MESH,
        ).wait_recv()

    def side(c):
        return pl.ds(c * half_c, half_c)

    def quad(h, c):
        for d in (2, 3, 1):
            send(
                O.at[h, d, :, side(c)], A.at[h, d, :, side(c)],
                s2s.at[h, c, d], s2r.at[h, c, d], expert_at(z, d), b,
            )

    def interleave(h, c):
        for d in (1, 2, 3):
            arrived(A.at[h, d, :, side(c)], s2s.at[h, c, d], s2r.at[h, c, d])
        r = lax.broadcasted_iota(jnp.int32, (64, 64), 0)
        q = lax.broadcasted_iota(jnp.int32, (64, 64), 1)
        origin = ((r >> 2) & 3) * 16 + ((r >> 4) & 3) * 4 + (r & 3)
        perm = (q == origin).astype(F32).astype(BF)
        step = 512

        @pl.loop(0, half_c // step)
        def _(t):
            cols = pl.ds(pl.multiple_of(c * half_c + t * step, step), step)
            rows = A[h, :, :, cols].reshape(64, step)
            moved = jnp.dot(perm, rows, preferred_element_type=F32).astype(BF)
            B[pl.ds(4 * h, 4), :, cols] = moved.reshape(4, 16, step)
            if h == 0:
                X[0, b, :, cols] = moved[:16]

    def along_z(h):
        for i in range(max(1, 4 * h), 4 * h + 4):
            send(
                B.at[i], X.at[i, b], s3s.at[i], s3r.at[i],
                ((z + NZ - STEPS[i]) % NZ) * NG + g, b,
            )

    right = ((x + 1) % NX) * 2
    left = ((x + NX - 1) % NX) * 2
    far = ((x + 2) % NX) * 2
    me = x * 2
    other = 1 - yh

    def go(i, block, slot, to, c=None):
        ref = X.at[i, block] if c is None else X.at[i, block, :, side(c)]
        send(ref, ref, xs.at[i, slot], xr.at[i, slot], e, to)

    def got(i, block, slot, c=None):
        ref = X.at[i, block] if c is None else X.at[i, block, :, side(c)]
        arrived(ref, xs.at[i, slot], xr.at[i, slot])

    def own_side(i, c):
        go(i, b, 0 + c, right + yh, c)
        go(i, b, 2 + c, left + yh, c)
        if i not in XFIRST:
            go(i, b, 4 + c, me + other, c)
        elif c == 1:
            go(i, b, 4, me + other)

    def own(i):
        arrived(X.at[i, b], s3s.at[i], s3r.at[i])
        if i in XFIRST:
            go(i, b, 4, me + other)
        go(i, b, 0, right + yh, 0)
        go(i, b, 3, left + yh, 1)
        if i not in XFIRST:
            go(i, b, 4, me + other, 0)
            go(i, b, 5, me + other, 1)
        go(i, b, 1, right + yh, 1)
        go(i, b, 2, left + yh, 0)

    def part(i):
        if i in XFIRST:
            return
        got(i, me + other, 4, 0)
        go(i, me + other, 6, right + other_row, 0)
        got(i, me + other, 5, 1)
        go(i, me + other, 9, left + other_row, 1)
        go(i, me + other, 7, right + other_row, 1)
        go(i, me + other, 8, left + other_row, 0)

    other_row = yh

    def onward(i):
        got(i, left + yh, 0, 0)
        go(i, left + yh, 10, right + yh, 0)
        got(i, right + yh, 3, 1)
        go(i, right + yh, 11, left + yh, 1)
        if i in XFIRST:
            got(i, left + yh, 1, 1)
            go(i, left + yh, 5, me + other)
            got(i, right + yh, 2, 0)
            go(i, right + yh, 6, me + other)
        else:
            got(i, left + other, 6, 0)
            go(i, left + other, 12, right + yh, 0)
            got(i, right + other, 9, 1)
            go(i, right + other, 13, left + yh, 1)

    def fin(i):
        got(i, far + yh, 10, 0)
        got(i, far + yh, 11, 1)
        if i in XFIRST:
            go(i, far + yh, 7, me + other)

    def done(i):
        if i in XFIRST:
            got(i, me + other, 4)
            got(i, left + other, 5)
            got(i, right + other, 6)
            got(i, far + other, 7)
        else:
            got(i, left + yh, 1, 1)
            got(i, right + yh, 2, 0)
            got(i, left + other, 7, 1)
            got(i, right + other, 8, 0)
            got(i, far + other, 12, 0)
            got(i, far + other, 13, 1)

    def h_ref(k, block, part_=None):
        i0, m = CHUNKS[k]
        if part_ is None:
            return H.at[pl.ds(i0, m), block]
        return H.at[pl.ds(i0, m), block, pl.ds(part_ * 64, 64)]

    def h_go(k, block, slot, to, part_=None):
        ref = h_ref(k, block, part_)
        send(ref, ref, hs.at[k, slot], hr.at[k, slot], e, to)

    def h_got(k, block, slot, part_=None):
        arrived(h_ref(k, block, part_), hs.at[k, slot], hr.at[k, slot])

    def h_own(k):
        if k in DIRECT:
            for j in (4, 3, 5, 2, 6, 1, 7):
                h_go(k, b, j, peer(j))
            return
        h_go(k, b, 2, me + other)
        h_go(k, b, 0, right + yh)
        h_go(k, b, 1, left + yh)

    def h_part(k):
        if k in DIRECT:
            return
        h_got(k, me + other, 2)
        h_go(k, me + other, 3, right + yh)
        h_go(k, me + other, 4, left + yh)

    def h_onward(k):
        if k in DIRECT:
            return
        h_got(k, left + yh, 0)
        h_go(k, left + yh, 5, right + yh, 0)
        h_got(k, right + yh, 1)
        h_go(k, right + yh, 6, left + yh, 1)
        h_got(k, left + other, 3)
        h_go(k, left + other, 7, right + yh, 0)
        h_got(k, right + other, 4)
        h_go(k, right + other, 8, left + yh, 1)

    def h_done(k):
        if k in DIRECT:
            for j in range(1, NB):
                h_got(k, peer(j), NB - j)
            return
        h_got(k, far + yh, 5, 0)
        h_got(k, far + yh, 6, 1)
        h_got(k, far + other, 7, 0)
        h_got(k, far + other, 8, 1)

    def gate_up(k):
        if k == 0:
            loads[3].wait()
            loads[4].wait()
        i0, m = CHUNKS[k]
        size = m * 128
        step = 1792

        @pl.loop(0, width // step)
        def _(t):
            cols = pl.ds(pl.multiple_of(t * step, step), step)
            rows = X[i0 : i0 + m, :, :, cols].reshape(size, step)
            term = jnp.dot(rows, WGU[cols, :], preferred_element_type=F32)

            @pl.when(t == 0)
            def _():
                acc[:size] = term

            @pl.when(t > 0)
            def _():
                acc[:size] += term

        gate, up = acc[:size, :half_w], acc[:size, half_w:]
        hidden = (gate / (1.0 + jnp.exp(-gate)) * up).astype(BF)
        H[i0 : i0 + m, b] = hidden.reshape(m, 128, half_w)

    def down(k):
        if k == 0:
            loads[5].wait()
        i0, m = CHUNKS[k]
        size = m * 128
        r = lax.broadcasted_iota(jnp.int32, (128, 128), 0)
        c = lax.broadcasted_iota(jnp.int32, (128, 128), 1)
        origin = ((r >> 2) & 7) * 16 + ((r >> 5) & 3) * 4 + (r & 3)
        perm = (c == origin).astype(F32).astype(BF)
        total = None
        for q in range(NB):
            term = jnp.dot(
                H[i0 : i0 + m, q].reshape(size, half_w),
                WD[q * half_w : (q + 1) * half_w, :],
                preferred_element_type=F32,
            )
            total = term if total is None else total + term
        rows = total.astype(BF)
        for u in range(m):
            i = i0 + u
            moved = jnp.dot(perm, rows[u * 128 : (u + 1) * 128], preferred_element_type=F32).astype(BF)
            Y[i] = moved.reshape(NG, 32, n)
            if i == 0:
                R[0, 0] = moved[:32]
            for d in (3, 2, 1, 0):
                if i or d:
                    send(
                        Y.at[i, d], R.at[i, d], rs.at[i, d], rr.at[i, d],
                        expert_at((z + STEPS[i]) % NZ, d), b,
                    )

    def weights():
        for j in range(1, NB):
            arrived(WT.at[peer(j)], ws.at[j], wr.at[NB - j])
        r = lax.broadcasted_iota(jnp.int32, (128, 1024), 0)
        c = lax.broadcasted_iota(jnp.int32, (128, 1024), 1)
        same = r == ((c >> 5) * 4 + (c & 3))

        @pl.loop(0, NB)
        def _(q):
            spread = jnp.where(same & (((c >> 2) & 7) == q), 1.0, 0.0).astype(BF)
            wide = jnp.dot(WT[q], spread, preferred_element_type=F32).astype(BF)
            WX[pl.ds(pl.multiple_of(q * 64, 64), 64), :] = wide

    def combine(k):
        i0, m = CHUNKS[k]
        for i in range(i0, i0 + m):
            for d in range(NG):
                if i or d:
                    arrived(R.at[i, d], rs.at[i, d], rr.at[i, d])
        part_ = WX[:, i0 * 128 : (i0 + m) * 128]
        term = jnp.dot(part_, R[i0 : i0 + m].reshape(m * 128, n), preferred_element_type=F32)
        if k == 0:
            pacc[...] = term
        elif k + 1 < len(CHUNKS):
            pacc[...] += term
        else:
            PB[...] = (pacc[...] + term).astype(BF).reshape(NB, 64, n)

    pack(0, 0)
    pl.semaphore_wait(barrier, NG - 1 + NZ - 1 + len(near))
    quad(0, 0)
    pack(0, 1)
    quad(0, 1)
    pack(1, 0)
    pack(1, 1)
    interleave(0, 0)
    own_side(0, 0)
    interleave(0, 1)
    own_side(0, 1)
    along_z(0)
    quad(1, 0)
    quad(1, 1)
    for copy in loads[3:]:
        copy.start()
    _, weighting = chosen_of(label_of(row >> 4, (row >> 2) & 3), row & 3)
    weighting = weighting.T.astype(BF)
    WO[...] = weighting
    WT[b] = weighting
    part(0)
    own(1)
    onward(0)
    interleave(1, 0)
    interleave(1, 1)
    along_z(1)
    part(1)
    own(2)
    own(3)
    part(2)
    for t in range(1, 9):
        if t + 3 < 8:
            own(t + 3)
        if t + 2 < 8:
            part(t + 2)
        if t < 8:
            onward(t)
        if t == 3:
            h_part(0)
        if t == 5:
            h_part(1)
        if t == 7:
            h_part(2)
        fin(t - 1)
        if t == 8:
            h_done(2)
            down(2)
        for i in range(8):
            if t == (i + 2 if i in XFIRST else i + 1):
                done(i)
        if t == 2:
            for j in range(1, NB):
                send(WO, WT.at[b], ws.at[j], wr.at[j], e, peer(j))
            gate_up(0)
            h_own(0)
        if t == 3:
            h_onward(0)
        if t == 4:
            gate_up(1)
            h_own(1)
            h_done(0)
            down(0)
            weights()
        if t == 5:
            h_onward(1)
        if t == 6:
            gate_up(2)
            h_own(2)
            h_done(1)
            down(1)
            combine(0)
        if t == 7:
            h_onward(2)
            gate_up(3)
            h_own(3)
        if t == 8:
            gate_up(4)
            h_own(4)
            combine(1)
            h_done(3)
            down(3)
            h_done(4)
            down(4)
    for k in range(2, 5):
        combine(k)
    for j in (4, 3, 5, 2, 6, 1, 7):
        send(PB.at[peer(j)], OB.at[b], fs.at[j], fr.at[j], e, peer(j))
    OB[b] = PB[b]
    for j in range(1, NB):
        arrived(OB.at[peer(j)], fs.at[j], fr.at[NB - j])
    for q in range(NB):
        out_ref[:, q * n : (q + 1) * n] = OB[q]
    for copy in sent:
        copy.wait_send()


def on_device(tokens, expert_ids, gate_weights, w_gate, w_up, w_down):
    tok, width = tokens.shape
    half_w = w_gate.shape[2]
    full_w, n = w_down.shape[1:]
    dma = pltpu.SemaphoreType.DMA
    any_ = pl.BlockSpec(memory_space=pl.ANY)
    units = NZ
    return pl.pallas_call(
        kernel,
        out_shape=jax.ShapeDtypeStruct((tok, width), BF),
        in_specs=[any_] * 6,
        out_specs=pl.BlockSpec(memory_space=pltpu.VMEM),
        scratch_shapes=[
            pltpu.VMEM((tok, width), BF),
            pltpu.VMEM(expert_ids.shape[::-1], jnp.int32),
            pltpu.VMEM(gate_weights.shape[::-1], BF),
            pltpu.VMEM((2, NG, 16, width), BF),
            pltpu.VMEM((2, NG, 16, width), BF),
            pltpu.VMEM((units, 16, width), BF),
            pltpu.VMEM((units, NB, 16, width), BF),
            pltpu.VMEM((units, NB, 128, half_w), BF),
            pltpu.VMEM((units, NG, 32, n), BF),
            pltpu.VMEM((units, NG, 32, n), BF),
            pltpu.VMEM((NB, tok, n), BF),
            pltpu.VMEM((NB, tok, n), BF),
            pltpu.VMEM((tok, 128), BF),
            pltpu.VMEM((NB, tok, 128), BF),
            pltpu.VMEM((NB * tok, 1024), BF),
            pltpu.VMEM((width, 2 * half_w), BF),
            pltpu.VMEM((full_w, n), BF),
            pltpu.VMEM((256, 2 * half_w), F32),
            pltpu.VMEM((NB * tok, n), F32),
            dma((6,)),
            dma((2, 2, NG)), dma((2, 2, NG)),
            dma((units,)), dma((units,)),
            dma((units, 14)), dma((units, 14)),
            dma((len(CHUNKS), 9)), dma((len(CHUNKS), 9)),
            dma((units, NG)), dma((units, NG)),
            dma((NB,)), dma((NB,)),
            dma((NB,)), dma((NB,)),
        ],
        compiler_params=pltpu.CompilerParams(
            collective_id=0, has_side_effects=True, vmem_limit_bytes=63 * 1024 * 1024
        ),
    )(tokens, expert_ids.T, gate_weights.T, w_gate[0], w_up[0], w_down[0])


def solution(mesh):
    return jax.shard_map(
        on_device,
        mesh=mesh,
        in_specs=(
            P(("expert", "blk"), None),
            P(("expert", "blk"), None),
            P(("expert", "blk"), None),
            P("expert", None, "blk"),
            P("expert", None, "blk"),
            P("expert", None, "blk"),
        ),
        out_specs=P(("expert", "blk"), None),
        check_vma=False,
    )
```

```python
import functools

import jax
import jax.numpy as jnp
from jax import lax
from jax.experimental import pallas as pl
from jax.experimental.pallas import tpu as pltpu
from jax.sharding import PartitionSpec as P

CAP = 4
MESH = pl.DeviceIdType.MESH
STEPS = (0, 1, 4, 5, 3, 6, 2, 7)
XFIRST = (2, 4)
CHUNKS = ((0, 2), (2, 2), (4, 2), (6, 1), (7, 1))
DIRECT = (3, 4)
HIDDEN_XFIRST = (0, 1)
NZ = 8
NG = 4
NX = 4
NB = 8
BF = jnp.bfloat16
F32 = jnp.float32


def kernel(
    tok_ref, ids_ref, gw_ref, wg_ref, wu_ref, wd_ref, out_ref,
    TK, IDS, GW, O, A, B, X, H, Y, R, PB, OB, WO, WT, WX, WGU, WD, acc, pacc,
    loc, s2s, s2r, s3s, s3r, xs, xr, hs, hr, rs, rr, ws, wr, fs, fr,
):
    e = lax.axis_index("expert")
    b = lax.axis_index("blk")
    z, g = e // NG, e % NG
    yl, co = g // 2, g % 2
    x, yh = b // 2, b % 2
    width = A.shape[-1]
    half_c = width // 2
    half_w = WGU.shape[1] // 2
    n = WD.shape[1]

    def expert_at(zz, d):
        return zz * NG + ((yl + d // 2) % 2) * 2 + (co + d % 2) % 2

    def peer(j):
        return (b + j) % NB

    barrier = pltpu.get_barrier_semaphore()
    loads = [
        pltpu.make_async_copy(ids_ref, IDS, loc.at[0]),
        pltpu.make_async_copy(gw_ref, GW, loc.at[1]),
        pltpu.make_async_copy(tok_ref, TK, loc.at[2]),
        pltpu.make_async_copy(wg_ref, WGU.at[:, pl.ds(0, half_w)], loc.at[3]),
        pltpu.make_async_copy(wu_ref, WGU.at[:, pl.ds(half_w, half_w)], loc.at[4]),
        pltpu.make_async_copy(wd_ref, WD, loc.at[5]),
    ]
    for copy in loads[:3]:
        copy.start()
    for d in range(1, NG):
        pl.semaphore_signal(barrier, inc=1, device_id=(expert_at(z, d), b), device_id_type=MESH)
    for i in range(1, NZ):
        pl.semaphore_signal(barrier, inc=1, device_id=((z + i) % NZ * NG + g, b), device_id_type=MESH)
    near = (((x + 1) % NX) * 2 + yh, ((x + NX - 1) % NX) * 2 + yh, x * 2 + 1 - yh)
    for block in near:
        pl.semaphore_signal(barrier, inc=1, device_id=(e, block), device_id_type=MESH)

    def label_of(unit, d):
        step = sum(jnp.where(unit == i, s, 0) for i, s in enumerate(STEPS))
        return ((z + NZ - step) & 7) * NG + ((yl + (d >> 1)) & 1) * 2 + ((co + d) & 1)

    def chosen_of(labels, place):
        ids = IDS[...]
        gate = GW[...].astype(F32)
        tok = ids.shape[1]
        hit = jnp.zeros((128, tok), F32)
        weight = jnp.zeros((128, tok), F32)
        for j in range(ids.shape[0]):
            match = ids[j : j + 1] == labels
            hit = jnp.where(match, 1.0, hit)
            weight = jnp.where(match, gate[j : j + 1], weight)
        r = lax.broadcasted_iota(jnp.int32, (tok, tok), 0)
        c = lax.broadcasted_iota(jnp.int32, (tok, tok), 1)
        earlier = jnp.where(r < c, 1.0, 0.0).astype(BF)
        before = jnp.dot(hit.astype(BF), earlier, preferred_element_type=F32)
        used = (hit > 0.5) & (before == place.astype(F32))
        return jnp.where(used, 1.0, 0.0), jnp.where(used, weight, 0.0)

    loads[0].wait()
    loads[1].wait()
    row = lax.broadcasted_iota(jnp.int32, (128, 1), 0)
    selector, _ = chosen_of(label_of((row >> 6) * 4 + ((row >> 2) & 3), (row >> 4) & 3), row & 3)
    selector = selector.astype(BF)
    loads[2].wait()

    def pack(h, c):
        step = 512

        @pl.loop(0, half_c // step)
        def _(t):
            cols = pl.ds(pl.multiple_of(c * half_c + t * step, step), step)
            rows = jnp.dot(selector[h * 64 : h * 64 + 64], TK[:, cols], preferred_element_type=F32)
            rows = rows.astype(BF).reshape(NG, 16, step)
            O[h, :, :, cols] = rows
            A[h, 0, :, cols] = rows[0]

    sent = []

    def send(src, dst, ss, rs_, ee, bb):
        copy = pltpu.make_async_remote_copy(
            src_ref=src, dst_ref=dst, send_sem=ss, recv_sem=rs_,
            device_id=(ee, bb), device_id_type=MESH,
        )
        copy.start()
        sent.append(copy)

    def arrived(dst, ss, rs_):
        pltpu.make_async_remote_copy(
            src_ref=dst, dst_ref=dst, send_sem=ss, recv_sem=rs_,
            device_id=(e, peer(1)), device_id_type=MESH,
        ).wait_recv()

    def side(c):
        return pl.ds(c * half_c, half_c)

    def quad(h, c):
        for d in (2, 3, 1):
            send(
                O.at[h, d, :, side(c)], A.at[h, d, :, side(c)],
                s2s.at[h, c, d], s2r.at[h, c, d], expert_at(z, d), b,
            )

    def interleave(h, c):
        for d in (1, 2, 3):
            arrived(A.at[h, d, :, side(c)], s2s.at[h, c, d], s2r.at[h, c, d])
        r = lax.broadcasted_iota(jnp.int32, (64, 64), 0)
        q = lax.broadcasted_iota(jnp.int32, (64, 64), 1)
        origin = ((r >> 2) & 3) * 16 + ((r >> 4) & 3) * 4 + (r & 3)
        perm = (q == origin).astype(F32).astype(BF)
        step = 512

        @pl.loop(0, half_c // step)
        def _(t):
            cols = pl.ds(pl.multiple_of(c * half_c + t * step, step), step)
            rows = A[h, :, :, cols].reshape(64, step)
            moved = jnp.dot(perm, rows, preferred_element_type=F32).astype(BF)
            B[pl.ds(4 * h, 4), :, cols] = moved.reshape(4, 16, step)
            if h == 0:
                X[0, b, :, cols] = moved[:16]

    def along_z(h):
        for i in range(max(1, 4 * h), 4 * h + 4):
            send(
                B.at[i], X.at[i, b], s3s.at[i], s3r.at[i],
                ((z + NZ - STEPS[i]) % NZ) * NG + g, b,
            )

    right = ((x + 1) % NX) * 2
    left = ((x + NX - 1) % NX) * 2
    far = ((x + 2) % NX) * 2
    me = x * 2
    other = 1 - yh

    def go(i, block, slot, to, c=None):
        ref = X.at[i, block] if c is None else X.at[i, block, :, side(c)]
        send(ref, ref, xs.at[i, slot], xr.at[i, slot], e, to)

    def got(i, block, slot, c=None):
        ref = X.at[i, block] if c is None else X.at[i, block, :, side(c)]
        arrived(ref, xs.at[i, slot], xr.at[i, slot])

    def own_side(i, c):
        go(i, b, 0 + c, right + yh, c)
        go(i, b, 2 + c, left + yh, c)
        if i not in XFIRST:
            go(i, b, 4 + c, me + other, c)
        elif c == 1:
            go(i, b, 4, me + other)

    def own(i):
        arrived(X.at[i, b], s3s.at[i], s3r.at[i])
        if i in XFIRST:
            go(i, b, 4, me + other)
        go(i, b, 0, right + yh, 0)
        go(i, b, 3, left + yh, 1)
        if i not in XFIRST:
            go(i, b, 4, me + other, 0)
            go(i, b, 5, me + other, 1)
        go(i, b, 1, right + yh, 1)
        go(i, b, 2, left + yh, 0)

    def part(i):
        if i in XFIRST:
            return
        got(i, me + other, 4, 0)
        go(i, me + other, 6, right + other_row, 0)
        got(i, me + other, 5, 1)
        go(i, me + other, 9, left + other_row, 1)
        go(i, me + other, 7, right + other_row, 1)
        go(i, me + other, 8, left + other_row, 0)

    other_row = yh

    def onward(i):
        got(i, left + yh, 0, 0)
        go(i, left + yh, 10, right + yh, 0)
        got(i, right + yh, 3, 1)
        go(i, right + yh, 11, left + yh, 1)
        if i in XFIRST:
            got(i, left + yh, 1, 1)
            go(i, left + yh, 5, me + other)
            got(i, right + yh, 2, 0)
            go(i, right + yh, 6, me + other)
        else:
            got(i, left + other, 6, 0)
            go(i, left + other, 12, right + yh, 0)
            got(i, right + other, 9, 1)
            go(i, right + other, 13, left + yh, 1)

    def fin(i):
        got(i, far + yh, 10, 0)
        got(i, far + yh, 11, 1)
        if i in XFIRST:
            go(i, far + yh, 7, me + other)

    def done(i):
        if i in XFIRST:
            got(i, me + other, 4)
            got(i, left + other, 5)
            got(i, right + other, 6)
            got(i, far + other, 7)
        else:
            got(i, left + yh, 1, 1)
            got(i, right + yh, 2, 0)
            got(i, left + other, 7, 1)
            got(i, right + other, 8, 0)
            got(i, far + other, 12, 0)
            got(i, far + other, 13, 1)

    def h_ref(k, block, part_=None):
        i0, m = CHUNKS[k]
        if part_ is None:
            return H.at[pl.ds(i0, m), block]
        return H.at[pl.ds(i0, m), block, pl.ds(part_ * 64, 64)]

    def h_go(k, block, slot, to, part_=None):
        ref = h_ref(k, block, part_)
        send(ref, ref, hs.at[k, slot], hr.at[k, slot], e, to)

    def h_got(k, block, slot, part_=None):
        arrived(h_ref(k, block, part_), hs.at[k, slot], hr.at[k, slot])

    def h_own(k):
        if k in DIRECT:
            for j in (4, 3, 5, 2, 6, 1, 7):
                h_go(k, b, j, peer(j))
            return
        h_go(k, b, 2, me + other)
        h_go(k, b, 0, right + yh)
        h_go(k, b, 1, left + yh)

    def h_part(k):
        if k in DIRECT or k in HIDDEN_XFIRST:
            return
        h_got(k, me + other, 2)
        h_go(k, me + other, 3, right + yh)
        h_go(k, me + other, 4, left + yh)

    def h_onward(k):
        if k in DIRECT:
            return
        h_got(k, left + yh, 0)
        h_go(k, left + yh, 5, right + yh, 0)
        h_got(k, right + yh, 1)
        h_go(k, right + yh, 6, left + yh, 1)
        if k in HIDDEN_XFIRST:
            h_go(k, left + yh, 3, me + other)
            h_go(k, right + yh, 4, me + other)
            return
        h_got(k, left + other, 3)
        h_go(k, left + other, 7, right + yh, 0)
        h_got(k, right + other, 4)
        h_go(k, right + other, 8, left + yh, 1)

    def h_fin(k):
        if k in HIDDEN_XFIRST:
            h_got(k, far + yh, 5, 0)
            h_got(k, far + yh, 6, 1)
            h_go(k, far + yh, 7, me + other)

    def h_done(k):
        if k in DIRECT:
            for j in range(1, NB):
                h_got(k, peer(j), NB - j)
            return
        if k in HIDDEN_XFIRST:
            h_got(k, me + other, 2)
            h_got(k, left + other, 3)
            h_got(k, right + other, 4)
            h_got(k, far + other, 7)
            return
        h_got(k, far + yh, 5, 0)
        h_got(k, far + yh, 6, 1)
        h_got(k, far + other, 7, 0)
        h_got(k, far + other, 8, 1)

    def gate_up(k):
        if k == 0:
            loads[3].wait()
            loads[4].wait()
        i0, m = CHUNKS[k]
        size = m * 128
        step = 1792

        @pl.loop(0, width // step)
        def _(t):
            cols = pl.ds(pl.multiple_of(t * step, step), step)
            rows = X[i0 : i0 + m, :, :, cols].reshape(size, step)
            term = jnp.dot(rows, WGU[cols, :], preferred_element_type=F32)

            @pl.when(t == 0)
            def _():
                acc[:size] = term

            @pl.when(t > 0)
            def _():
                acc[:size] += term

        gate, up = acc[:size, :half_w], acc[:size, half_w:]
        hidden = (gate / (1.0 + jnp.exp(-gate)) * up).astype(BF)
        H[i0 : i0 + m, b] = hidden.reshape(m, 128, half_w)

    def down(k):
        if k == 0:
            loads[5].wait()
        i0, m = CHUNKS[k]
        size = m * 128
        r = lax.broadcasted_iota(jnp.int32, (128, 128), 0)
        c = lax.broadcasted_iota(jnp.int32, (128, 128), 1)
        origin = ((r >> 2) & 7) * 16 + ((r >> 5) & 3) * 4 + (r & 3)
        perm = (c == origin).astype(F32).astype(BF)
        total = None
        for q in range(NB):
            term = jnp.dot(
                H[i0 : i0 + m, q].reshape(size, half_w),
                WD[q * half_w : (q + 1) * half_w, :],
                preferred_element_type=F32,
            )
            total = term if total is None else total + term
        rows = total.astype(BF)
        for u in range(m):
            i = i0 + u
            moved = jnp.dot(perm, rows[u * 128 : (u + 1) * 128], preferred_element_type=F32).astype(BF)
            Y[i] = moved.reshape(NG, 32, n)
            if i == 0:
                R[0, 0] = moved[:32]
            for d in (3, 2, 1, 0):
                if i or d:
                    send(
                        Y.at[i, d], R.at[i, d], rs.at[i, d], rr.at[i, d],
                        expert_at((z + STEPS[i]) % NZ, d), b,
                    )

    def weights():
        for j in range(1, NB):
            arrived(WT.at[peer(j)], ws.at[j], wr.at[NB - j])
        r = lax.broadcasted_iota(jnp.int32, (128, 1024), 0)
        c = lax.broadcasted_iota(jnp.int32, (128, 1024), 1)
        same = r == ((c >> 5) * 4 + (c & 3))

        @pl.loop(0, NB)
        def _(q):
            spread = jnp.where(same & (((c >> 2) & 7) == q), 1.0, 0.0).astype(BF)
            wide = jnp.dot(WT[q], spread, preferred_element_type=F32).astype(BF)
            WX[pl.ds(pl.multiple_of(q * 64, 64), 64), :] = wide

    def combine(k):
        i0, m = CHUNKS[k]
        for i in range(i0, i0 + m):
            for d in range(NG):
                if i or d:
                    arrived(R.at[i, d], rs.at[i, d], rr.at[i, d])
        part_ = WX[:, i0 * 128 : (i0 + m) * 128]
        term = jnp.dot(part_, R[i0 : i0 + m].reshape(m * 128, n), preferred_element_type=F32)
        if k == 0:
            pacc[...] = term
        elif k + 1 < len(CHUNKS):
            pacc[...] += term
        else:
            PB[...] = (pacc[...] + term).astype(BF).reshape(NB, 64, n)

    pack(0, 0)
    pl.semaphore_wait(barrier, NG - 1 + NZ - 1 + len(near))
    quad(0, 0)
    pack(0, 1)
    quad(0, 1)
    pack(1, 0)
    pack(1, 1)
    interleave(0, 0)
    own_side(0, 0)
    interleave(0, 1)
    own_side(0, 1)
    along_z(0)
    quad(1, 0)
    quad(1, 1)
    for copy in loads[3:]:
        copy.start()
    _, weighting = chosen_of(label_of(row >> 4, (row >> 2) & 3), row & 3)
    weighting = weighting.T.astype(BF)
    WO[...] = weighting
    WT[b] = weighting
    part(0)
    own(1)
    onward(0)
    interleave(1, 0)
    interleave(1, 1)
    along_z(1)
    part(1)
    own(2)
    own(3)
    part(2)
    for t in range(1, 9):
        if t + 3 < 8:
            own(t + 3)
        if t + 2 < 8:
            part(t + 2)
        if t < 8:
            onward(t)
        if t == 3:
            h_part(0)
        if t == 5:
            h_part(1)
        if t == 7:
            h_part(2)
        fin(t - 1)
        if t == 8:
            h_fin(2)
            h_done(2)
            down(2)
        for i in range(8):
            if t == (i + 2 if i in XFIRST else i + 1):
                done(i)
        if t == 2:
            for j in range(1, NB):
                send(WO, WT.at[b], ws.at[j], wr.at[j], e, peer(j))
            gate_up(0)
            h_own(0)
        if t == 3:
            h_onward(0)
        if t == 4:
            h_fin(0)
            gate_up(1)
            h_own(1)
            h_done(0)
            down(0)
            weights()
        if t == 5:
            h_onward(1)
        if t == 6:
            h_fin(1)
            gate_up(2)
            h_own(2)
            h_done(1)
            down(1)
            combine(0)
        if t == 7:
            h_onward(2)
            gate_up(3)
            h_own(3)
        if t == 8:
            gate_up(4)
            h_own(4)
            combine(1)
            h_done(3)
            down(3)
            h_done(4)
            down(4)
    for k in range(2, 5):
        combine(k)
    for j in (4, 3, 5, 2, 6, 1, 7):
        send(PB.at[peer(j)], OB.at[b], fs.at[j], fr.at[j], e, peer(j))
    OB[b] = PB[b]
    for j in range(1, NB):
        arrived(OB.at[peer(j)], fs.at[j], fr.at[NB - j])
    for q in range(NB):
        out_ref[:, q * n : (q + 1) * n] = OB[q]
    for copy in sent:
        copy.wait_send()


def on_device(tokens, expert_ids, gate_weights, w_gate, w_up, w_down):
    tok, width = tokens.shape
    half_w = w_gate.shape[2]
    full_w, n = w_down.shape[1:]
    dma = pltpu.SemaphoreType.DMA
    any_ = pl.BlockSpec(memory_space=pl.ANY)
    units = NZ
    return pl.pallas_call(
        kernel,
        out_shape=jax.ShapeDtypeStruct((tok, width), BF),
        in_specs=[any_] * 6,
        out_specs=pl.BlockSpec(memory_space=pltpu.VMEM),
        scratch_shapes=[
            pltpu.VMEM((tok, width), BF),
            pltpu.VMEM(expert_ids.shape[::-1], jnp.int32),
            pltpu.VMEM(gate_weights.shape[::-1], BF),
            pltpu.VMEM((2, NG, 16, width), BF),
            pltpu.VMEM((2, NG, 16, width), BF),
            pltpu.VMEM((units, 16, width), BF),
            pltpu.VMEM((units, NB, 16, width), BF),
            pltpu.VMEM((units, NB, 128, half_w), BF),
            pltpu.VMEM((units, NG, 32, n), BF),
            pltpu.VMEM((units, NG, 32, n), BF),
            pltpu.VMEM((NB, tok, n), BF),
            pltpu.VMEM((NB, tok, n), BF),
            pltpu.VMEM((tok, 128), BF),
            pltpu.VMEM((NB, tok, 128), BF),
            pltpu.VMEM((NB * tok, 1024), BF),
            pltpu.VMEM((width, 2 * half_w), BF),
            pltpu.VMEM((full_w, n), BF),
            pltpu.VMEM((256, 2 * half_w), F32),
            pltpu.VMEM((NB * tok, n), F32),
            dma((6,)),
            dma((2, 2, NG)), dma((2, 2, NG)),
            dma((units,)), dma((units,)),
            dma((units, 14)), dma((units, 14)),
            dma((len(CHUNKS), 9)), dma((len(CHUNKS), 9)),
            dma((units, NG)), dma((units, NG)),
            dma((NB,)), dma((NB,)),
            dma((NB,)), dma((NB,)),
        ],
        compiler_params=pltpu.CompilerParams(
            collective_id=0, has_side_effects=True, vmem_limit_bytes=63 * 1024 * 1024
        ),
    )(tokens, expert_ids.T, gate_weights.T, w_gate[0], w_up[0], w_down[0])


def solution(mesh):
    return jax.shard_map(
        on_device,
        mesh=mesh,
        in_specs=(
            P(("expert", "blk"), None),
            P(("expert", "blk"), None),
            P(("expert", "blk"), None),
            P("expert", None, "blk"),
            P("expert", None, "blk"),
            P("expert", None, "blk"),
        ),
        out_specs=P(("expert", "blk"), None),
        check_vma=False,
    )
```

```python
import functools

import jax
import jax.numpy as jnp
from jax import lax
from jax.experimental import pallas as pl
from jax.experimental.pallas import tpu as pltpu
from jax.sharding import PartitionSpec as P

CAP = 4
MESH = pl.DeviceIdType.MESH
STEPS = (0, 1, 4, 5, 3, 6, 2, 7)
XFIRST = (2, 4)
CHUNKS = ((0, 2), (2, 2), (4, 2), (6, 1), (7, 1))
DIRECT = (3, 4)
HIDDEN_XFIRST = (0, 1)
NZ = 8
NG = 4
NX = 4
NB = 8
BF = jnp.bfloat16
F32 = jnp.float32


def kernel(
    tok_ref, ids_ref, gw_ref, wg_ref, wu_ref, wd_ref, out_ref,
    TK, IDS, GW, O, A, B, X, H, Y, R, PB, OB, WO, WT, WX, WGU, WD, acc, pacc,
    loc, s2s, s2r, s3s, s3r, xs, xr, hs, hr, rs, rr, ws, wr, fs, fr,
):
    e = lax.axis_index("expert")
    b = lax.axis_index("blk")
    z, g = e // NG, e % NG
    yl, co = g // 2, g % 2
    x, yh = b // 2, b % 2
    width = A.shape[-1]
    half_c = width // 2
    half_w = WGU.shape[1] // 2
    n = WD.shape[1]

    def expert_at(zz, d):
        return zz * NG + ((yl + d // 2) % 2) * 2 + (co + d % 2) % 2

    def peer(j):
        return (b + j) % NB

    barrier = pltpu.get_barrier_semaphore()
    loads = [
        pltpu.make_async_copy(ids_ref, IDS, loc.at[0]),
        pltpu.make_async_copy(gw_ref, GW, loc.at[1]),
        pltpu.make_async_copy(tok_ref, TK, loc.at[2]),
        pltpu.make_async_copy(wg_ref, WGU.at[:, pl.ds(0, half_w)], loc.at[3]),
        pltpu.make_async_copy(wu_ref, WGU.at[:, pl.ds(half_w, half_w)], loc.at[4]),
        pltpu.make_async_copy(wd_ref, WD, loc.at[5]),
    ]
    for copy in loads[:3]:
        copy.start()
    for d in range(1, NG):
        pl.semaphore_signal(barrier, inc=1, device_id=(expert_at(z, d), b), device_id_type=MESH)
    for i in range(1, NZ):
        pl.semaphore_signal(barrier, inc=1, device_id=((z + i) % NZ * NG + g, b), device_id_type=MESH)
    near = (((x + 1) % NX) * 2 + yh, ((x + NX - 1) % NX) * 2 + yh, x * 2 + 1 - yh)
    for block in near:
        pl.semaphore_signal(barrier, inc=1, device_id=(e, block), device_id_type=MESH)

    def label_of(unit, d):
        step = sum(jnp.where(unit == i, s, 0) for i, s in enumerate(STEPS))
        return ((z + NZ - step) & 7) * NG + ((yl + (d >> 1)) & 1) * 2 + ((co + d) & 1)

    def chosen_of(labels, place):
        ids = IDS[...]
        gate = GW[...].astype(F32)
        tok = ids.shape[1]
        hit = jnp.zeros((128, tok), F32)
        weight = jnp.zeros((128, tok), F32)
        for j in range(ids.shape[0]):
            match = ids[j : j + 1] == labels
            hit = jnp.where(match, 1.0, hit)
            weight = jnp.where(match, gate[j : j + 1], weight)
        r = lax.broadcasted_iota(jnp.int32, (tok, tok), 0)
        c = lax.broadcasted_iota(jnp.int32, (tok, tok), 1)
        earlier = jnp.where(r < c, 1.0, 0.0).astype(BF)
        before = jnp.dot(hit.astype(BF), earlier, preferred_element_type=F32)
        used = (hit > 0.5) & (before == place.astype(F32))
        return jnp.where(used, 1.0, 0.0), jnp.where(used, weight, 0.0)

    loads[0].wait()
    loads[1].wait()
    row = lax.broadcasted_iota(jnp.int32, (128, 1), 0)
    selector, _ = chosen_of(label_of((row >> 6) * 4 + ((row >> 2) & 3), (row >> 4) & 3), row & 3)
    selector = selector.astype(BF)
    loads[2].wait()

    def pack(h, c):
        step = 512

        @pl.loop(0, half_c // step)
        def _(t):
            cols = pl.ds(pl.multiple_of(c * half_c + t * step, step), step)
            rows = jnp.dot(selector[h * 64 : h * 64 + 64], TK[:, cols], preferred_element_type=F32)
            rows = rows.astype(BF).reshape(NG, 16, step)
            O[h, :, :, cols] = rows
            A[h, 0, :, cols] = rows[0]

    sent = []

    def send(src, dst, ss, rs_, ee, bb):
        copy = pltpu.make_async_remote_copy(
            src_ref=src, dst_ref=dst, send_sem=ss, recv_sem=rs_,
            device_id=(ee, bb), device_id_type=MESH,
        )
        copy.start()
        sent.append(copy)

    def arrived(dst, ss, rs_):
        pltpu.make_async_remote_copy(
            src_ref=dst, dst_ref=dst, send_sem=ss, recv_sem=rs_,
            device_id=(e, peer(1)), device_id_type=MESH,
        ).wait_recv()

    def side(c):
        return pl.ds(c * half_c, half_c)

    def quad(h, c):
        for d in (2, 3, 1):
            send(
                O.at[h, d, :, side(c)], A.at[h, d, :, side(c)],
                s2s.at[h, c, d], s2r.at[h, c, d], expert_at(z, d), b,
            )

    def interleave(h, c):
        for d in (1, 2, 3):
            arrived(A.at[h, d, :, side(c)], s2s.at[h, c, d], s2r.at[h, c, d])
        r = lax.broadcasted_iota(jnp.int32, (64, 64), 0)
        q = lax.broadcasted_iota(jnp.int32, (64, 64), 1)
        origin = ((r >> 2) & 3) * 16 + ((r >> 4) & 3) * 4 + (r & 3)
        perm = (q == origin).astype(F32).astype(BF)
        step = 512

        @pl.loop(0, half_c // step)
        def _(t):
            cols = pl.ds(pl.multiple_of(c * half_c + t * step, step), step)
            rows = A[h, :, :, cols].reshape(64, step)
            moved = jnp.dot(perm, rows, preferred_element_type=F32).astype(BF)
            B[pl.ds(4 * h, 4), :, cols] = moved.reshape(4, 16, step)
            if h == 0:
                X[0, b, :, cols] = moved[:16]

    def along_z(h):
        for i in range(max(1, 4 * h), 4 * h + 4):
            send(
                B.at[i], X.at[i, b], s3s.at[i], s3r.at[i],
                ((z + NZ - STEPS[i]) % NZ) * NG + g, b,
            )

    right = ((x + 1) % NX) * 2
    left = ((x + NX - 1) % NX) * 2
    far = ((x + 2) % NX) * 2
    me = x * 2
    other = 1 - yh

    def go(i, block, slot, to, c=None):
        ref = X.at[i, block] if c is None else X.at[i, block, :, side(c)]
        send(ref, ref, xs.at[i, slot], xr.at[i, slot], e, to)

    def got(i, block, slot, c=None):
        ref = X.at[i, block] if c is None else X.at[i, block, :, side(c)]
        arrived(ref, xs.at[i, slot], xr.at[i, slot])

    def own_side(i, c):
        go(i, b, 0 + c, right + yh, c)
        go(i, b, 2 + c, left + yh, c)
        if i not in XFIRST:
            go(i, b, 4 + c, me + other, c)
        elif c == 1:
            go(i, b, 4, me + other)

    def own(i):
        arrived(X.at[i, b], s3s.at[i], s3r.at[i])
        if i in XFIRST:
            go(i, b, 4, me + other)
        go(i, b, 0, right + yh, 0)
        go(i, b, 3, left + yh, 1)
        if i not in XFIRST:
            go(i, b, 4, me + other, 0)
            go(i, b, 5, me + other, 1)
        go(i, b, 1, right + yh, 1)
        go(i, b, 2, left + yh, 0)

    def part(i):
        if i in XFIRST:
            return
        got(i, me + other, 4, 0)
        go(i, me + other, 6, right + other_row, 0)
        got(i, me + other, 5, 1)
        go(i, me + other, 9, left + other_row, 1)
        go(i, me + other, 7, right + other_row, 1)
        go(i, me + other, 8, left + other_row, 0)

    other_row = yh

    def onward(i):
        got(i, left + yh, 0, 0)
        go(i, left + yh, 10, right + yh, 0)
        got(i, right + yh, 3, 1)
        go(i, right + yh, 11, left + yh, 1)
        if i in XFIRST:
            got(i, left + yh, 1, 1)
            go(i, left + yh, 5, me + other)
            got(i, right + yh, 2, 0)
            go(i, right + yh, 6, me + other)
        else:
            got(i, left + other, 6, 0)
            go(i, left + other, 12, right + yh, 0)
            got(i, right + other, 9, 1)
            go(i, right + other, 13, left + yh, 1)

    def fin(i):
        got(i, far + yh, 10, 0)
        got(i, far + yh, 11, 1)
        if i in XFIRST:
            go(i, far + yh, 7, me + other)

    def done(i):
        if i in XFIRST:
            got(i, me + other, 4)
            got(i, left + other, 5)
            got(i, right + other, 6)
            got(i, far + other, 7)
        else:
            got(i, left + yh, 1, 1)
            got(i, right + yh, 2, 0)
            got(i, left + other, 7, 1)
            got(i, right + other, 8, 0)
            got(i, far + other, 12, 0)
            got(i, far + other, 13, 1)

    def h_ref(k, block, part_=None):
        i0, m = CHUNKS[k]
        if part_ is None:
            return H.at[pl.ds(i0, m), block]
        return H.at[pl.ds(i0, m), block, pl.ds(part_ * 64, 64)]

    def h_go(k, block, slot, to, part_=None):
        ref = h_ref(k, block, part_)
        send(ref, ref, hs.at[k, slot], hr.at[k, slot], e, to)

    def h_got(k, block, slot, part_=None):
        arrived(h_ref(k, block, part_), hs.at[k, slot], hr.at[k, slot])

    def h_own(k):
        if k in DIRECT:
            for j in (4, 3, 5, 2, 6, 1, 7):
                h_go(k, b, j, peer(j))
            return
        h_go(k, b, 2, me + other)
        h_go(k, b, 0, right + yh)
        h_go(k, b, 1, left + yh)

    def h_part(k):
        if k in DIRECT or k in HIDDEN_XFIRST:
            return
        h_got(k, me + other, 2)
        h_go(k, me + other, 3, right + yh)
        h_go(k, me + other, 4, left + yh)

    def h_onward(k):
        if k in DIRECT:
            return
        h_got(k, left + yh, 0)
        h_go(k, left + yh, 5, right + yh, 0)
        h_got(k, right + yh, 1)
        h_go(k, right + yh, 6, left + yh, 1)
        if k in HIDDEN_XFIRST:
            h_go(k, left + yh, 3, me + other)
            h_go(k, right + yh, 4, me + other)
            return
        h_got(k, left + other, 3)
        h_go(k, left + other, 7, right + yh, 0)
        h_got(k, right + other, 4)
        h_go(k, right + other, 8, left + yh, 1)

    def h_fin(k):
        if k in HIDDEN_XFIRST:
            h_got(k, far + yh, 5, 0)
            h_got(k, far + yh, 6, 1)
            h_go(k, far + yh, 7, me + other)

    def h_done(k):
        if k in DIRECT:
            for j in range(1, NB):
                h_got(k, peer(j), NB - j)
            return
        if k in HIDDEN_XFIRST:
            h_got(k, me + other, 2)
            h_got(k, left + other, 3)
            h_got(k, right + other, 4)
            h_got(k, far + other, 7)
            return
        h_got(k, far + yh, 5, 0)
        h_got(k, far + yh, 6, 1)
        h_got(k, far + other, 7, 0)
        h_got(k, far + other, 8, 1)

    def gate_up(k):
        if k == 0:
            loads[3].wait()
            loads[4].wait()
        i0, m = CHUNKS[k]
        size = m * 128
        step = 1792

        @pl.loop(0, width // step)
        def _(t):
            cols = pl.ds(pl.multiple_of(t * step, step), step)
            rows = X[i0 : i0 + m, :, :, cols].reshape(size, step)
            term = jnp.dot(rows, WGU[cols, :], preferred_element_type=F32)

            @pl.when(t == 0)
            def _():
                acc[:size] = term

            @pl.when(t > 0)
            def _():
                acc[:size] += term

        gate, up = acc[:size, :half_w], acc[:size, half_w:]
        hidden = (gate / (1.0 + jnp.exp(-gate)) * up).astype(BF)
        H[i0 : i0 + m, b] = hidden.reshape(m, 128, half_w)

    def down(k):
        if k == 0:
            loads[5].wait()
        i0, m = CHUNKS[k]
        size = m * 128
        r = lax.broadcasted_iota(jnp.int32, (128, 128), 0)
        c = lax.broadcasted_iota(jnp.int32, (128, 128), 1)
        origin = ((r >> 2) & 7) * 16 + ((r >> 5) & 3) * 4 + (r & 3)
        perm = (c == origin).astype(F32).astype(BF)
        total = None
        for q in range(NB):
            term = jnp.dot(
                H[i0 : i0 + m, q].reshape(size, half_w),
                WD[q * half_w : (q + 1) * half_w, :],
                preferred_element_type=F32,
            )
            total = term if total is None else total + term
        rows = total.astype(BF)
        for u in range(m):
            i = i0 + u
            moved = jnp.dot(perm, rows[u * 128 : (u + 1) * 128], preferred_element_type=F32).astype(BF)
            Y[i] = moved.reshape(NG, 32, n)
            if i == 0:
                R[0, 0] = moved[:32]
            for d in (3, 2, 1, 0):
                if i or d:
                    send(
                        Y.at[i, d], R.at[i, d], rs.at[i, d], rr.at[i, d],
                        expert_at((z + STEPS[i]) % NZ, d), b,
                    )

    def weights():
        for j in range(1, NB):
            arrived(WT.at[peer(j)], ws.at[j], wr.at[NB - j])
        r = lax.broadcasted_iota(jnp.int32, (128, 1024), 0)
        c = lax.broadcasted_iota(jnp.int32, (128, 1024), 1)
        same = r == ((c >> 5) * 4 + (c & 3))

        @pl.loop(0, NB)
        def _(q):
            spread = jnp.where(same & (((c >> 2) & 7) == q), 1.0, 0.0).astype(BF)
            wide = jnp.dot(WT[q], spread, preferred_element_type=F32).astype(BF)
            WX[pl.ds(pl.multiple_of(q * 64, 64), 64), :] = wide

    def combine(k):
        i0, m = CHUNKS[k]
        for i in range(i0, i0 + m):
            for d in range(NG):
                if i or d:
                    arrived(R.at[i, d], rs.at[i, d], rr.at[i, d])
        part_ = WX[:, i0 * 128 : (i0 + m) * 128]
        term = jnp.dot(part_, R[i0 : i0 + m].reshape(m * 128, n), preferred_element_type=F32)
        if k == 0:
            pacc[...] = term
        elif k + 1 < len(CHUNKS):
            pacc[...] += term
        else:
            PB[...] = (pacc[...] + term).astype(BF).reshape(NB, 64, n)

    pack(0, 0)
    pl.semaphore_wait(barrier, NG - 1 + NZ - 1 + len(near))
    quad(0, 0)
    pack(0, 1)
    quad(0, 1)
    pack(1, 0)
    pack(1, 1)
    interleave(0, 0)
    own_side(0, 0)
    interleave(0, 1)
    own_side(0, 1)
    along_z(0)
    quad(1, 0)
    quad(1, 1)
    for copy in loads[3:]:
        copy.start()
    _, weighting = chosen_of(label_of(row >> 4, (row >> 2) & 3), row & 3)
    weighting = weighting.T.astype(BF)
    WO[...] = weighting
    WT[b] = weighting
    part(0)
    own(1)
    onward(0)
    interleave(1, 0)
    interleave(1, 1)
    along_z(1)
    part(1)
    own(2)
    for t in range(1, 9):
        if t + 2 < 8:
            own(t + 2)
        if t + 1 < 8:
            part(t + 1)
        if t < 8:
            onward(t)
        if t == 3:
            h_part(0)
        if t == 5:
            h_part(1)
        if t == 7:
            h_part(2)
        fin(t - 1)
        if t == 8:
            h_fin(2)
            h_done(2)
            down(2)
        for i in range(8):
            if t == (i + 2 if i in XFIRST else i + 1):
                done(i)
        if t == 2:
            for j in range(1, NB):
                send(WO, WT.at[b], ws.at[j], wr.at[j], e, peer(j))
            gate_up(0)
            h_own(0)
        if t == 3:
            h_onward(0)
        if t == 4:
            h_fin(0)
            gate_up(1)
            h_own(1)
            h_done(0)
            down(0)
            weights()
        if t == 5:
            h_onward(1)
        if t == 6:
            h_fin(1)
            gate_up(2)
            h_own(2)
            h_done(1)
            down(1)
            combine(0)
        if t == 7:
            h_onward(2)
            gate_up(3)
            h_own(3)
        if t == 8:
            gate_up(4)
            h_own(4)
            combine(1)
            h_done(3)
            down(3)
            h_done(4)
            down(4)
    for k in range(2, 5):
        combine(k)
    for j in (4, 3, 5, 2, 6, 1, 7):
        send(PB.at[peer(j)], OB.at[b], fs.at[j], fr.at[j], e, peer(j))
    OB[b] = PB[b]
    for j in range(1, NB):
        arrived(OB.at[peer(j)], fs.at[j], fr.at[NB - j])
    for q in range(NB):
        out_ref[:, q * n : (q + 1) * n] = OB[q]
    for copy in sent:
        copy.wait_send()


def on_device(tokens, expert_ids, gate_weights, w_gate, w_up, w_down):
    tok, width = tokens.shape
    half_w = w_gate.shape[2]
    full_w, n = w_down.shape[1:]
    dma = pltpu.SemaphoreType.DMA
    any_ = pl.BlockSpec(memory_space=pl.ANY)
    units = NZ
    return pl.pallas_call(
        kernel,
        out_shape=jax.ShapeDtypeStruct((tok, width), BF),
        in_specs=[any_] * 6,
        out_specs=pl.BlockSpec(memory_space=pltpu.VMEM),
        scratch_shapes=[
            pltpu.VMEM((tok, width), BF),
            pltpu.VMEM(expert_ids.shape[::-1], jnp.int32),
            pltpu.VMEM(gate_weights.shape[::-1], BF),
            pltpu.VMEM((2, NG, 16, width), BF),
            pltpu.VMEM((2, NG, 16, width), BF),
            pltpu.VMEM((units, 16, width), BF),
            pltpu.VMEM((units, NB, 16, width), BF),
            pltpu.VMEM((units, NB, 128, half_w), BF),
            pltpu.VMEM((units, NG, 32, n), BF),
            pltpu.VMEM((units, NG, 32, n), BF),
            pltpu.VMEM((NB, tok, n), BF),
            pltpu.VMEM((NB, tok, n), BF),
            pltpu.VMEM((tok, 128), BF),
            pltpu.VMEM((NB, tok, 128), BF),
            pltpu.VMEM((NB * tok, 1024), BF),
            pltpu.VMEM((width, 2 * half_w), BF),
            pltpu.VMEM((full_w, n), BF),
            pltpu.VMEM((256, 2 * half_w), F32),
            pltpu.VMEM((NB * tok, n), F32),
            dma((6,)),
            dma((2, 2, NG)), dma((2, 2, NG)),
            dma((units,)), dma((units,)),
            dma((units, 14)), dma((units, 14)),
            dma((len(CHUNKS), 9)), dma((len(CHUNKS), 9)),
            dma((units, NG)), dma((units, NG)),
            dma((NB,)), dma((NB,)),
            dma((NB,)), dma((NB,)),
        ],
        compiler_params=pltpu.CompilerParams(
            collective_id=0, has_side_effects=True, vmem_limit_bytes=63 * 1024 * 1024
        ),
    )(tokens, expert_ids.T, gate_weights.T, w_gate[0], w_up[0], w_down[0])


def solution(mesh):
    return jax.shard_map(
        on_device,
        mesh=mesh,
        in_specs=(
            P(("expert", "blk"), None),
            P(("expert", "blk"), None),
            P(("expert", "blk"), None),
            P("expert", None, "blk"),
            P("expert", None, "blk"),
            P("expert", None, "blk"),
        ),
        out_specs=P(("expert", "blk"), None),
        check_vma=False,
    )
```
